256 devices in a mesh: dp: 2 (over core), row: 16 (over y, x), col: 8 (over z).
Axes of the slice: x: 4, y: 4, z: 8, core: 2. Of those that a mesh axis runs over, the one named last changes fastest.
Arguments:
- features: bfloat16 [2, 256, 128, 1024], P('dp', None, 'row', 'col'), may hold values from -41 to 41, as said below
- group_kernel: bfloat16 [256, 72], replicated, may hold values from -0.75 to 0.75
- norm_gain: float32 [256], replicated, may hold values from 0.1 to 1.9
- norm_bias: float32 [256], replicated, may hold values from -3 to 3
- mix_weight: bfloat16 [256, 256], replicated, may hold values from -0.375 to 0.375
- cotangent: bfloat16 [2, 256, 128, 1024], P('dp', None, 'row', 'col'), may hold values from -6 to 6
Outputs:
- mixed: bfloat16 [2, 256, 128, 1024], P('dp', None, 'row', 'col')
- grad_features: bfloat16 [2, 256, 128, 1024], P('dp', None, 'row', 'col')
- grad_mix: float32 [256, 256], replicated
- grad_gain: float32 [256], replicated
- grad_bias: float32 [256], replicated
- grad_kernel: float32 [256, 72], replicated
- grad_whiten: float32 [2, 256, 256], P('dp')
The draws below stay inside these ranges and needn't reach their ends.
Inputs may be any that keep to these rules, and one draw needn't show every extreme that they name: `features`: feature maps whose scale varies over channels and over cells.
All inputs are finite; a program needn't handle non-finite values.
Results may differ from the reference program's by a relative error of at most 0.0085.
Values may be sent and summed in bfloat16 or wider, within the bound.
A program may use at most 64 MiB of HBM per device.

```python
import jax
import jax.numpy as jnp
from jax import lax

CH = 256
GROUPS = 32
GW = 8
NEWTON = 5
SCENES = 2
ROWS = 128
COLS = 1024


def draw_features(key, part):
    key_base = jax.random.fold_in(key, 11)
    key_chan = jax.random.fold_in(key, 12)
    key_cell = jax.random.fold_in(key, 13)
    shape = (SCENES, CH, ROWS, COLS)
    chan_scale = jnp.exp(jax.random.uniform(key_chan, (CH,), jnp.float32, jnp.log(0.3), jnp.log(3.0)))
    cell_scale = jnp.exp(jax.random.uniform(key_cell, (SCENES, 1, ROWS, COLS), jnp.float32, jnp.log(0.3), jnp.log(3.0)))
    row_frac = jnp.arange(ROWS, dtype=jnp.float32) / max(ROWS - 1, 1)
    col_frac = jnp.arange(COLS, dtype=jnp.float32) / max(COLS - 1, 1)
    ramp = 0.5 * jnp.power(3.0, 0.5 * (row_frac[:, None] + col_frac[None, :]))
    base = jax.random.truncated_normal(key_base, -3.0, 3.0, shape, jnp.float32)
    values = base * chan_scale[None, :, None, None] * cell_scale * ramp[None, None, :, :]
    return values.astype(jnp.bfloat16)


def levels(rng, extent, cuts, smallest, top_value):
    def one(dim, blocks):
        steps = jax.random.uniform(jax.random.fold_in(jax.random.fold_in(rng, 6), dim), (blocks,), jnp.float32, smallest / len(cuts), top_value / len(cuts))
        return jnp.repeat(jnp.exp(steps), extent[dim] // blocks).reshape((-1,) + (1,) * (len(extent) - dim - 1))

    level = one(*cuts[0])
    for cut in cuts[1:]:
        level = level * one(*cut)
    return level


def bell_draw(own_key, extent, scale, reach, cuts=(), kind=jnp.bfloat16):
    array = jax.random.normal(own_key, extent, jnp.float32) * scale
    if len(cuts) > 0:
        array = levels(own_key, extent, cuts, -0.22, 0.18) * array
    return jnp.clip(array, min=-reach, max=reach).astype(kind)


def setup_inputs(seed: int = 0) -> dict:
    splits = jax.random.split(jax.random.key(seed), 7)
    features = draw_features(jax.random.fold_in(splits[6], 71), 0)
    group_kernel = bell_draw(splits[1], (CH, GW * 9), (GW * 9) ** -0.5, 0.75)
    norm_gain = jnp.clip(1.0 + 0.18 * jax.random.normal(splits[2], (CH,), jnp.float32), 0.1, 1.9)
    norm_bias = bell_draw(splits[3], (CH,), 0.5, 3.0, (), jnp.float32)
    mix_weight = bell_draw(splits[4], (CH, CH), CH ** -0.5, 0.375)
    cotangent = bell_draw(splits[5], (SCENES, CH, ROWS, COLS), 1.0, 6.0, ((0, 2), (2, 16), (3, 8)))
    return dict(features=features, group_kernel=group_kernel, norm_gain=norm_gain, norm_bias=norm_bias, mix_weight=mix_weight, cotangent=cotangent)


EPS = 1e-05

def group_conv(padded, kernel):
    chans, prow, pcol = padded.shape
    height = prow - 2
    width = pcol - 2
    gwidth = chans // GROUPS
    pieces = padded.reshape(GROUPS, gwidth, prow, pcol).astype(jnp.float32)
    weights = kernel.reshape(GROUPS, gwidth, gwidth, 9).astype(jnp.float32)
    total = jnp.zeros((GROUPS, gwidth, height, width), jnp.float32)
    for position in range(9):
        shift_row, shift_col = divmod(position, 3)
        window = pieces[:, :, shift_row:shift_row + height, shift_col:shift_col + width]
        total = total + jnp.einsum('goi,girw->gorw', weights[..., position], window, precision=lax.Precision.HIGHEST)
    return total.reshape(chans, height, width)

def conv_transpose(grad_pad, kernel):
    chans, prow, pcol = grad_pad.shape
    height = prow - 2
    width = pcol - 2
    gwidth = chans // GROUPS
    pieces = grad_pad.reshape(GROUPS, gwidth, prow, pcol).astype(jnp.float32)
    weights = kernel.reshape(GROUPS, gwidth, gwidth, 9).astype(jnp.float32)
    total = jnp.zeros((GROUPS, gwidth, height, width), jnp.float32)
    for position in range(9):
        shift_row, shift_col = divmod(position, 3)
        window = pieces[:, :, 2 - shift_row:2 - shift_row + height, 2 - shift_col:2 - shift_col + width]
        total = total + jnp.einsum('goi,gorw->girw', weights[..., position], window, precision=lax.Precision.HIGHEST)
    return total.reshape(chans, height, width)

def kernel_grad(grad_conv, padded):
    chans, height, width = grad_conv.shape
    gwidth = chans // GROUPS
    grads = grad_conv.reshape(GROUPS, gwidth, height, width).astype(jnp.float32)
    pieces = padded.reshape(GROUPS, gwidth, height + 2, width + 2).astype(jnp.float32)
    parts = []
    for position in range(9):
        shift_row, shift_col = divmod(position, 3)
        window = pieces[:, :, shift_row:shift_row + height, shift_col:shift_col + width]
        parts.append(jnp.einsum('gorw,girw->goi', grads, window, precision=lax.Precision.HIGHEST))
    return jnp.stack(parts, axis=-1).reshape(chans, gwidth * 9)

def whitening(covariance):
    trace_value = jnp.trace(covariance)
    normed = covariance / trace_value
    proj = jnp.eye(covariance.shape[0], dtype=covariance.dtype)
    for step in range(NEWTON):
        cube = jnp.dot(jnp.dot(proj, proj, precision=lax.Precision.HIGHEST), proj, precision=lax.Precision.HIGHEST)
        proj = 0.5 * (3.0 * proj - jnp.dot(cube, normed, precision=lax.Precision.HIGHEST))
    return proj / jnp.sqrt(trace_value)

def one_scene(image, grad_out, kernel, norm_gain, norm_bias, mix_weight):
    chans, height, width = image.shape
    cells = height * width
    padded = jnp.pad(image, ((0, 0), (1, 1), (1, 1)))
    conv = group_conv(padded, kernel).astype(jnp.bfloat16)
    flat = conv.reshape(chans, cells).astype(jnp.float32)
    channel_mean = lax.optimization_barrier(jnp.mean(flat, axis=1))
    centered = flat - channel_mean[:, None]
    eye_mat = jnp.eye(chans, dtype=centered.dtype)
    covariance = jnp.dot(centered, centered.T, precision=lax.Precision.HIGHEST) / cells + EPS * eye_mat
    whiten = whitening(covariance)
    normed = jnp.dot(whiten, centered, precision=lax.Precision.HIGHEST)
    shifted = norm_gain[:, None] * normed + norm_bias[:, None]
    gate = jax.nn.sigmoid(shifted)
    act = (shifted * gate).astype(jnp.bfloat16)
    mixed = (image.reshape(chans, cells).astype(jnp.float32) + jnp.dot(mix_weight, act, preferred_element_type=jnp.float32)).astype(jnp.bfloat16)
    upstream = grad_out.reshape(chans, cells)
    dact = jnp.dot(mix_weight.T, upstream, preferred_element_type=jnp.float32)
    dshift = dact * gate * (1.0 + shifted * (1.0 - gate))
    grad_mix = jnp.dot(upstream, act.T, preferred_element_type=jnp.float32)
    grad_gain = lax.optimization_barrier(jnp.sum(dshift * normed, axis=1))
    grad_bias = lax.optimization_barrier(jnp.sum(dshift, axis=1))
    dnormed = (norm_gain[:, None] * dshift).astype(jnp.bfloat16).astype(jnp.float32)
    grad_sum = lax.optimization_barrier(jnp.sum(dnormed, axis=1))
    dwhiten = jnp.dot(dnormed, flat.T, precision=lax.Precision.HIGHEST) - jnp.outer(grad_sum, channel_mean)
    white_out = dwhiten / jnp.sqrt(jnp.float32(cells))
    unused, pullback = jax.vjp(whitening, covariance)
    dcov = pullback(dwhiten)[0]
    dsym = 0.5 * (dcov + dcov.T)
    dconv = jnp.dot(whiten.T, dnormed - (grad_sum / cells)[:, None], precision=lax.Precision.HIGHEST)
    dconv = (dconv + jnp.dot(dsym * (2.0 / cells), centered, precision=lax.Precision.HIGHEST)).astype(jnp.bfloat16)
    dconv = dconv.reshape(chans, height, width)
    grad_pad = jnp.pad(dconv, ((0, 0), (1, 1), (1, 1)))
    grad_image = (grad_out.astype(jnp.float32) + conv_transpose(grad_pad, kernel)).astype(jnp.bfloat16)
    grad_ker = kernel_grad(dconv, padded)
    return (mixed.reshape(chans, height, width), grad_image, white_out, grad_mix, grad_gain, grad_bias, grad_ker)

def reference(features, group_kernel, norm_gain, norm_bias, mix_weight, cotangent):
    outs_mixed = []
    outs_grad = []
    outs_white = []
    sums = None
    for index in range(SCENES):
        result = one_scene(features[index], cotangent[index], group_kernel, norm_gain, norm_bias, mix_weight)
        outs_mixed.append(result[0])
        outs_grad.append(result[1])
        outs_white.append(result[2])
        if sums is None:
            sums = list(result[3:])
        else:
            sums = [acc + part for acc, part in zip(sums, result[3:])]
    scale = 1.0 / jnp.sqrt(jnp.float32(SCENES * ROWS * COLS))
    return (jnp.stack(outs_mixed), jnp.stack(outs_grad), sums[0] * scale, sums[1] * scale, sums[2] * scale, sums[3] * scale, jnp.stack(outs_white))
```

```python
import functools

import jax
import jax.numpy as jnp
from jax import lax
from jax.experimental import pallas as pl
from jax.experimental.pallas import tpu as pltpu
from jax.sharding import PartitionSpec as P

GROUPS = 32
NEWTON = 5
EPS = 1e-05
MESH = pl.DeviceIdType.MESH
F32 = jnp.float32
BF16 = jnp.bfloat16

NN = (((1,), (0,)), ((), ()))
NT = (((1,), (1,)), ((), ()))
TN = (((0,), (0,)), ((), ()))

SIDES = ((0, -1), (0, 1), (-1, -1), (-1, 1), (1, -1), (1, 1))


def mm(a, b, dims=NN):
    return lax.dot_general(a, b, dims, preferred_element_type=F32)


def split(a):
    high = a.astype(BF16)
    return high, (a - high.astype(F32)).astype(BF16)


def mm3(a, b):
    ah, al = split(a)
    bh, bl = split(b)
    return mm(jnp.concatenate([ah, ah, al], axis=1), jnp.concatenate([bh, bl, bh], axis=0))


def iota(shape, dim):
    return lax.broadcasted_iota(jnp.int32, shape, dim)


def eye_mask(n):
    return iota((n, n), 0) == iota((n, n), 1)


def to_col(row):
    n = row.shape[1]
    return jnp.sum(jnp.where(eye_mask(n), row, 0.0), axis=1, keepdims=True)


def to_row(col):
    n = col.shape[0]
    return jnp.sum(jnp.where(eye_mask(n), col, 0.0), axis=0, keepdims=True)


def kernel(
    dims,
    feat,
    kern,
    gain,
    bias,
    mix,
    cot,
    mixed_out,
    gfeat_out,
    gmix_out,
    ggain_out,
    gbias_out,
    gker_out,
    gwhite_out,
    kpad,
    kst,
    ktst,
    xpad,
    dpad,
    xedge,
    dedge,
    xrows,
    drows,
    xside,
    dside,
    conv,
    dact,
    act,
    dnorm,
    dconv,
    gacc,
    bacc,
    send1,
    recv1,
    csend1,
    crecv1,
    cov,
    send2,
    recv2,
    csend2,
    crecv2,
    white,
    send3,
    recv3,
    csend3,
    crecv3,
    gmix,
    send4,
    recv4,
    csend4,
    crecv4,
    gker,
    hsems,
    rs_s,
    rs_r,
    cx_s,
    cx_r,
    ag_s,
    ag_r,
):
    ndp, nrow, ncol, height, width = dims
    chans = feat.shape[0]
    gwidth = chans // GROUPS
    cells = height * width
    total = cells * nrow * ncol
    chunk = chans // nrow
    nwide = ndp * ncol
    block = 2 * width
    nblk = cells // block
    dp = lax.axis_index("dp")
    row = lax.axis_index("row")
    col = lax.axis_index("col")

    def row_peer(k):
        return (dp, lax.rem(row + k, nrow), col)

    def col_peer(k):
        return (dp, row, lax.rem(col + k, ncol))

    def wide_peer(k):
        slot = lax.rem(dp * ncol + col + k, nwide)
        return (slot // ncol, row, lax.rem(slot, ncol))

    def side_peer(step):
        return (
            dp,
            lax.rem(row + step[0] + nrow, nrow),
            lax.rem(col + step[1] + ncol, ncol),
        )

    barrier = pltpu.get_barrier_semaphore()

    def greet(peer):
        pl.semaphore_signal(barrier, inc=1, device_id=peer, device_id_type=MESH)

    @pl.loop(1, nrow)
    def _(k):
        greet(row_peer(k))

    @pl.loop(1, nwide)
    def _(k):
        greet(wide_peer(k))

    for step in SIDES[2:]:
        greet(side_peer(step))

    kpad[...] = jnp.zeros_like(kpad)
    kpad[:, : 9 * gwidth] = kern[...]
    own_group = (iota((chans, chans), 0) // gwidth) == (iota((chans, chans), 1) // gwidth)

    def pick(tap):
        tapcol = iota((128, chans), 0)
        within = lax.rem(iota((128, chans), 1), gwidth)
        return (tapcol == 9 * within + tap).astype(F32).astype(BF16)

    @pl.loop(0, 9)
    def _(tap):
        dense = jnp.where(own_group, mm(kpad[...], pick(tap)), 0.0)
        kst[:, pl.ds(pl.multiple_of(tap * chans, chans), chans)] = dense.astype(BF16)
        ktst[:, pl.ds(pl.multiple_of((8 - tap) * chans, chans), chans)] = dense.T.astype(BF16)

    def edges(source, edge):
        index = iota((2 * height, cells), 0)
        cell = jnp.where(index < height, index * width, (index - height) * width + width - 1)
        chosen = (iota((2 * height, cells), 1) == cell).astype(F32).astype(BF16)
        edge[...] = mm(chosen, source[...], NT).astype(BF16)

    def halo_copies(source, edge, rows, sides, base):
        copies = []
        for slot, (step, lanes) in enumerate(
            (((1, 0), pl.ds(cells - width, width)), ((-1, 0), pl.ds(0, width)))
        ):
            copies.append(
                pltpu.make_async_remote_copy(
                    src_ref=source.at[:, lanes],
                    dst_ref=rows.at[slot],
                    send_sem=hsems.at[base + slot],
                    recv_sem=hsems.at[base + 8 + slot],
                    device_id=side_peer(step),
                    device_id_type=MESH,
                )
            )
        for slot, step in enumerate(SIDES):
            copies.append(
                pltpu.make_async_remote_copy(
                    src_ref=edge,
                    dst_ref=sides.at[slot],
                    send_sem=hsems.at[base + 2 + slot],
                    recv_sem=hsems.at[base + 10 + slot],
                    device_id=side_peer((-step[0], -step[1])),
                    device_id_type=MESH,
                )
            )
        return copies

    has_up, has_down = row > 0, row < nrow - 1
    has_left, has_right = col > 0, col < ncol - 1

    def fill(source, rows, sides, pad):
        pad[1, :, width : width + cells] = source[...]
        up = jnp.where(has_up, 1.0, 0.0)
        down = jnp.where(has_down, 1.0, 0.0)
        pad[1, :, 0:width] = (rows[0].astype(F32) * up).astype(BF16)
        pad[1, :, width + cells :] = (rows[1].astype(F32) * down).astype(BF16)
        side = sides[...].reshape(8 * 2 * height, chans).astype(F32)
        live = iota((8 * 2 * height, chans), 0) < 6 * 2 * height
        side = jnp.where(live, side, 0.0).T.astype(BF16)
        tall = 2 * height

        @pl.loop(0, height + 2)
        def _(tile):
            lanes = pl.ds(pl.multiple_of(tile * width, width), width)
            value = pad[1, :, lanes].astype(F32)
            lane = iota((chans, width), 1)
            first, last = tile == 0, tile == height + 1
            vertical = jnp.logical_or(
                jnp.logical_and(first, has_up),
                jnp.logical_or(
                    jnp.logical_and(last, has_down),
                    jnp.logical_and(tile > 0, tile < height + 1),
                ),
            )
            kleft = jnp.where(
                first, 2 * tall + tall - 1, jnp.where(last, 4 * tall + height, height + tile - 1)
            )
            kright = jnp.where(
                first, 3 * tall + height - 1, jnp.where(last, 5 * tall, tall + tile - 1)
            )
            kleft = jnp.where(jnp.logical_and(vertical, has_left), kleft, -1)
            kright = jnp.where(jnp.logical_and(vertical, has_right), kright, -1)
            which = iota((8 * tall, 2 * width), 0)
            where = iota((8 * tall, 2 * width), 1)
            place = jnp.where(where == 0, kleft, jnp.where(where == 2 * width - 1, kright, -2))
            brought = mm(side, (which == place).astype(F32).astype(BF16))
            left = jnp.where(lane == 0, 0.0, pltpu.roll(value, 1, 1)) + brought[:, :width]
            right = (
                jnp.where(lane == width - 1, 0.0, pltpu.roll(value, width - 1, 1))
                + brought[:, width:]
            )
            pad[0, :, lanes] = left.astype(BF16)
            pad[2, :, lanes] = right.astype(BF16)

    def window(pad, tap, start, size):
        shift_row, shift_col = divmod(tap, 3)
        return pad[shift_col, :, pl.ds(pl.multiple_of(start + shift_row * width, width), size)]

    edges(feat, xedge)
    pl.semaphore_wait(barrier, (nrow - 1) + (nwide - 1) + 4)
    halo1 = halo_copies(feat, xedge, xrows, xside, 0)
    for copy in halo1:
        copy.start()

    @pl.loop(0, nblk)
    def _(n):
        lanes = pl.ds(pl.multiple_of(n * block, block), block)
        dact[:, lanes] = mm(mix[...], cot[:, lanes], TN)

    for copy in halo1:
        copy.wait_recv()

    fill(feat, xrows, xside, xpad)

    @pl.loop(0, nblk)
    def _(n):
        lanes = pl.ds(pl.multiple_of(n * block, block), block)
        taps = [window(xpad, tap, n * block, block) for tap in range(9)]
        conv[:, lanes] = mm(kst[...], jnp.concatenate(taps, axis=0)).astype(BF16)

    ones = jnp.ones((16, cells), BF16)

    def pack(send, full, source):
        sums = mm(ones, source[...], NT)[:8]

        for j in range(nrow):
            send[j, :chunk] = full[j * chunk : (j + 1) * chunk]
            send[j, chunk:] = sums

    def scatter(red, send, recv):
        def make(k, slot):
            return pltpu.make_async_remote_copy(
                src_ref=send.at[lax.rem(row + k, nrow)],
                dst_ref=recv.at[slot],
                send_sem=rs_s.at[red, k],
                recv_sem=rs_r.at[red, k],
                device_id=row_peer(k),
                device_id_type=MESH,
            )

        return make

    def scatter_start(red, send, recv):
        make = scatter(red, send, recv)

        @pl.loop(1, nrow)
        def _(k):
            make(k, row).start()

        recv[row] = send[row]

    def scatter_wait(red, send, recv):
        make = scatter(red, send, recv)

        @pl.loop(1, nrow)
        def _(k):
            make(k, lax.rem(row - k + nrow, nrow)).wait_recv()

        value = recv[0]
        for j in range(1, nrow):
            value = value + recv[j]
        return value

    def exchange(red, csend, crecv, wide):
        count = nwide if wide else ncol
        mine = dp * ncol + col if wide else col

        def make(k, slot):
            return pltpu.make_async_remote_copy(
                src_ref=csend,
                dst_ref=crecv.at[slot],
                send_sem=cx_s.at[red, k],
                recv_sem=cx_r.at[red, k],
                device_id=wide_peer(k) if wide else col_peer(k),
                device_id_type=MESH,
            )

        return make, count, mine

    def exchange_start(red, csend, crecv, wide, value):
        make, count, mine = exchange(red, csend, crecv, wide)
        csend[...] = value

        @pl.loop(1, count)
        def _(k):
            make(k, mine).start()

        crecv[mine] = value

    def exchange_wait(red, csend, crecv, wide):
        make, count, mine = exchange(red, csend, crecv, wide)

        @pl.loop(1, count)
        def _(k):
            make(k, lax.rem(mine - k + count, count)).wait_recv()

        value = crecv[0]
        for j in range(1, count):
            value = value + crecv[j]
        return value

    def gather(red, full):
        def make(k, owner):
            rows = pl.ds(pl.multiple_of(owner * chunk, chunk), chunk)
            return pltpu.make_async_remote_copy(
                src_ref=full.at[rows],
                dst_ref=full.at[rows],
                send_sem=ag_s.at[red, k],
                recv_sem=ag_r.at[red, k],
                device_id=row_peer(k),
                device_id_type=MESH,
            )

        return make

    def gather_start(red, full, value):
        make = gather(red, full)
        full[pl.ds(pl.multiple_of(row * chunk, chunk), chunk)] = value

        @pl.loop(1, nrow)
        def _(k):
            make(k, row).start()

    def gather_wait(red, full):
        make = gather(red, full)

        @pl.loop(1, nrow)
        def _(k):
            make(k, lax.rem(row - k + nrow, nrow)).wait_recv()

    def chunk_col(line):
        at = iota((chunk, chans), 1) == iota((chunk, chans), 0) + row * chunk
        return jnp.sum(jnp.where(at, line, 0.0), axis=1, keepdims=True)

    pack(send1, mm(conv[...], conv[...], NT), conv)
    scatter_start(0, send1, recv1)
    exchange_start(0, csend1, crecv1, False, scatter_wait(0, send1, recv1))
    moments = exchange_wait(0, csend1, crecv1, False)
    mean = moments[chunk : chunk + 1] * (1.0 / total)
    at_diag = iota((chunk, chans), 1) == iota((chunk, chans), 0) + row * chunk
    piece = moments[:chunk] * (1.0 / total) - chunk_col(mean) * mean
    gather_start(0, cov, piece + jnp.where(at_diag, EPS, 0.0))
    gather_wait(0, cov)

    diag = eye_mask(chans)
    trace = jnp.sum(
        jnp.sum(jnp.where(diag, cov[...], 0.0), axis=1, keepdims=True), axis=0, keepdims=True
    )
    inv_trace = 1.0 / trace
    inv_root = lax.rsqrt(trace)
    normal = cov[...] * inv_trace
    projs = [jnp.where(diag, 1.5, 0.0) - 0.5 * normal]
    squares, mixes = [], []
    for _ in range(1, NEWTON):
        proj = projs[-1]
        squares.append(mm3(proj, proj))
        mixes.append(mm3(proj, normal))
        projs.append(1.5 * proj - 0.5 * mm3(squares[-1], mixes[-1]))
    whiten = projs[-1] * inv_root
    wmean = jnp.sum(whiten * mean, axis=1, keepdims=True)
    whigh, wlow = split(whiten)
    wpair = jnp.concatenate([whigh, wlow], axis=1)
    gain_col = to_col(gain[...])
    bias_col = to_col(bias[...])

    gacc[...] = jnp.zeros_like(gacc)
    bacc[...] = jnp.zeros_like(bacc)

    @pl.loop(0, nblk)
    def _(n):
        lanes = pl.ds(pl.multiple_of(n * block, block), block)
        here = conv[:, lanes]
        normed = mm(wpair, jnp.concatenate([here, here], axis=0)) - wmean
        shifted = gain_col * normed + bias_col
        gate = jax.nn.sigmoid(shifted)
        act[:, lanes] = (shifted * gate).astype(BF16)
        dshift = dact[:, lanes] * gate * (1.0 + shifted * (1.0 - gate))
        dnorm[:, lanes] = (gain_col * dshift).astype(BF16)
        weighted = dshift * normed
        gacc[...] += weighted[:, :width] + weighted[:, width:]
        bacc[...] += dshift[:, :width] + dshift[:, width:]

    pack(send2, mm(dnorm[...], conv[...], NT), dnorm)
    scatter_start(1, send2, recv2)

    @pl.loop(0, nblk)
    def _(n):
        lanes = pl.ds(pl.multiple_of(n * block, block), block)
        added = feat[:, lanes].astype(F32) + mm(mix[...], act[:, lanes])
        mixed_out[:, lanes] = added.astype(BF16)

    exchange_start(1, csend2, crecv2, False, scatter_wait(1, send2, recv2))
    mix_part = mm(cot[...], act[...], NT)

    for j in range(nrow):
        send3[j] = mix_part[j * chunk : (j + 1) * chunk]

    sums2 = exchange_wait(1, csend2, crecv2, False)
    grad_sum = sums2[chunk : chunk + 1]
    gather_start(1, white, sums2[:chunk] - chunk_col(grad_sum) * mean)
    gather_wait(1, white)
    scatter_start(2, send3, recv3)

    dwhiten = white[...]
    gwhite_out[...] = dwhiten * (1.0 / float(total) ** 0.5)
    sym = 0.5 * (dwhiten + dwhiten.T)
    dproj = -0.5 * sym
    for k in range(NEWTON - 1):
        proj, square, mixp = projs[k], squares[k], mixes[k]
        dsquare = mm3(dproj, proj)
        dsquare = dsquare + dsquare.T
        dmix = mm3(dproj, normal) + mm3(proj, sym)
        dproj = 1.5 * dproj - 0.5 * (mm3(dsquare, mixp) + mm3(square, dmix))

    def full_sum(value):
        return jnp.sum(jnp.sum(value, axis=1, keepdims=True), axis=0, keepdims=True)

    scalar = full_sum(sym * projs[-1]) * 0.5 + full_sum(dproj * normal)
    dsym = inv_trace * inv_root * (dproj - jnp.where(diag, scalar, 0.0))
    dsym = (dsym + dsym.T) * (1.0 / total)
    exchange_start(2, csend3, crecv3, True, scatter_wait(2, send3, recv3))

    shift_col = (
        jnp.sum(whiten * grad_sum, axis=1, keepdims=True) * (1.0 / total)
        + jnp.sum(dsym * mean, axis=1, keepdims=True)
    )
    dhigh, dlow = split(dsym)
    quad = jnp.concatenate([whigh, wlow, dhigh, dlow], axis=1)

    @pl.loop(0, nblk)
    def _(n):
        lanes = pl.ds(pl.multiple_of(n * block, block), block)
        one, two = dnorm[:, lanes], conv[:, lanes]
        value = mm(quad, jnp.concatenate([one, one, two, two], axis=0)) - shift_col
        dconv[:, lanes] = value.astype(BF16)

    edges(dconv, dedge)
    halo2 = halo_copies(dconv, dedge, drows, dside, 16)
    for copy in halo2:
        copy.start()

    lane = iota((chans, 128), 1)
    gker_cols = jnp.where(
        lane == 9 * gwidth,
        jnp.sum(gacc[...], axis=1, keepdims=True),
        jnp.where(lane == 9 * gwidth + 1, jnp.sum(bacc[...], axis=1, keepdims=True), 0.0),
    )
    gacc[...] = gker_cols

    for tap in range(9):
        dense = mm(dconv[...], window(xpad, tap, 0, cells), NT)
        high, low = split(jnp.where(own_group, dense, 0.0))
        gacc[...] += mm(high, pick(tap), NT) + mm(low, pick(tap), NT)

    for j in range(nrow):
        send4[j] = gacc[j * chunk : (j + 1) * chunk]

    scatter_start(3, send4, recv4)
    scale = 1.0 / float(ndp * total) ** 0.5
    gather_start(2, gmix, exchange_wait(2, csend3, crecv3, True) * scale)

    for copy in halo2:
        copy.wait_recv()
    exchange_start(3, csend4, crecv4, True, scatter_wait(3, send4, recv4))
    fill(dconv, drows, dside, dpad)
    gather_start(3, gker, exchange_wait(3, csend4, crecv4, True) * scale)

    @pl.loop(0, nblk)
    def _(n):
        lanes = pl.ds(pl.multiple_of(n * block, block), block)
        taps = [window(dpad, tap, n * block, block) for tap in range(9)]
        value = mm(ktst[...], jnp.concatenate(taps, axis=0))
        gfeat_out[:, lanes] = (cot[:, lanes].astype(F32) + value).astype(BF16)

    gather_wait(2, gmix)
    gmix_out[...] = gmix[...]
    gather_wait(3, gker)
    final = gker[...]
    gker_out[...] = final[:, : 9 * gwidth]
    ggain_out[...] = to_row(final[:, 9 * gwidth : 9 * gwidth + 1])
    gbias_out[...] = to_row(final[:, 9 * gwidth + 1 : 9 * gwidth + 2])

    for copy in halo1 + halo2:
        copy.wait_send()
    for red, (send, recv, csend, crecv, full) in enumerate(
        (
            (send1, recv1, csend1, crecv1, cov),
            (send2, recv2, csend2, crecv2, white),
            (send3, recv3, csend3, crecv3, gmix),
            (send4, recv4, csend4, crecv4, gker),
        )
    ):
        one, three = scatter(red, send, recv), gather(red, full)
        two, count, mine = exchange(red, csend, crecv, red > 1)

        @pl.loop(1, nrow)
        def _(k):
            one(k, row).wait_send()
            three(k, row).wait_send()

        @pl.loop(1, count)
        def _(k):
            two(k, mine).wait_send()


def solution(mesh):
    ndp, nrow, ncol = (mesh.shape[name] for name in ("dp", "row", "col"))

    def local(features, group_kernel, norm_gain, norm_bias, mix_weight, cotangent):
        chans, height, width = features.shape[1:]
        cells = height * width
        chunk = chans // nrow
        nwide = ndp * ncol
        padded = cells + 2 * width

        def reduction(rows, cols, wide):
            return [
                pltpu.VMEM((nrow, rows, cols), F32),
                pltpu.VMEM((nrow, rows, cols), F32),
                pltpu.VMEM((rows, cols), F32),
                pltpu.VMEM((nwide if wide else ncol, rows, cols), F32),
                pltpu.VMEM((chans, cols), F32),
            ]

        vmem = pl.BlockSpec(memory_space=pltpu.VMEM)
        outs = pl.pallas_call(
            functools.partial(kernel, (ndp, nrow, ncol, height, width)),
            out_shape=(
                jax.ShapeDtypeStruct((chans, cells), BF16),
                jax.ShapeDtypeStruct((chans, cells), BF16),
                jax.ShapeDtypeStruct((chans, chans), F32),
                jax.ShapeDtypeStruct((1, chans), F32),
                jax.ShapeDtypeStruct((1, chans), F32),
                jax.ShapeDtypeStruct(group_kernel.shape, F32),
                jax.ShapeDtypeStruct((chans, chans), F32),
            ),
            in_specs=[vmem] * 6,
            out_specs=[vmem] * 7,
            scratch_shapes=[
                pltpu.VMEM((chans, 128), BF16),
                pltpu.VMEM((chans, 9 * chans), BF16),
                pltpu.VMEM((chans, 9 * chans), BF16),
                pltpu.VMEM((3, chans, padded), BF16),
                pltpu.VMEM((3, chans, padded), BF16),
                pltpu.VMEM((2 * height, chans), BF16),
                pltpu.VMEM((2 * height, chans), BF16),
                pltpu.VMEM((2, chans, width), BF16),
                pltpu.VMEM((2, chans, width), BF16),
                pltpu.VMEM((8, 2 * height, chans), BF16),
                pltpu.VMEM((8, 2 * height, chans), BF16),
                pltpu.VMEM((chans, cells), BF16),
                pltpu.VMEM((chans, cells), F32),
                pltpu.VMEM((chans, cells), BF16),
                pltpu.VMEM((chans, cells), BF16),
                pltpu.VMEM((chans, cells), BF16),
                pltpu.VMEM((chans, 128), F32),
                pltpu.VMEM((chans, 128), F32),
                *reduction(chunk + 8, chans, False),
                *reduction(chunk + 8, chans, False),
                *reduction(chunk, chans, True),
                *reduction(chunk, 128, True),
                pltpu.SemaphoreType.DMA((32,)),
                pltpu.SemaphoreType.DMA((4, nrow)),
                pltpu.SemaphoreType.DMA((4, nrow)),
                pltpu.SemaphoreType.DMA((4, nwide)),
                pltpu.SemaphoreType.DMA((4, nwide)),
                pltpu.SemaphoreType.DMA((4, nrow)),
                pltpu.SemaphoreType.DMA((4, nrow)),
            ],
            compiler_params=pltpu.CompilerParams(
                collective_id=0, has_side_effects=True, vmem_limit_bytes=60 * 1024 * 1024
            ),
        )(
            features.reshape(chans, cells),
            group_kernel,
            norm_gain.reshape(1, chans),
            norm_bias.reshape(1, chans),
            mix_weight,
            cotangent.reshape(chans, cells),
        )
        mixed, gfeat, gmix, ggain, gbias, gker, gwhite = outs
        return (
            mixed.reshape(features.shape),
            gfeat.reshape(features.shape),
            gmix,
            ggain.reshape(chans),
            gbias.reshape(chans),
            gker,
            gwhite[None],
        )

    in_specs = (P("dp", None, "row", "col"), P(), P(), P(), P(), P("dp", None, "row", "col"))
    out_specs = (
        P("dp", None, "row", "col"),
        P("dp", None, "row", "col"),
        P(),
        P(),
        P(),
        P(),
        P("dp", None, None),
    )
    return jax.shard_map(local, mesh=mesh, in_specs=in_specs, out_specs=out_specs, check_vma=False)
```

```python
import functools
import math

import jax
import jax.numpy as jnp
from jax import lax
from jax.experimental import pallas as pl
from jax.experimental.pallas import tpu as pltpu
from jax.sharding import PartitionSpec as P

GROUPS = 32
NEWTON = 5
EPS = 1e-05
MESH = pl.DeviceIdType.MESH
F32 = jnp.float32
BF16 = jnp.bfloat16

NN = (((1,), (0,)), ((), ()))
NT = (((1,), (1,)), ((), ()))
TN = (((0,), (0,)), ((), ()))

SIDES = ((0, -1), (0, 1), (-1, -1), (-1, 1), (1, -1), (1, 1))


def mm(a, b, dims=NN):
    return lax.dot_general(a, b, dims, preferred_element_type=F32)


def split(a):
    high = a.astype(BF16)
    return high, (a - high.astype(F32)).astype(BF16)


def mm3(a, b):
    ah, al = split(a)
    bh, bl = split(b)
    return mm(jnp.concatenate([ah, ah, al], axis=1), jnp.concatenate([bh, bl, bh], axis=0))


def iota(shape, dim):
    return lax.broadcasted_iota(jnp.int32, shape, dim)


def eye_mask(n):
    return iota((n, n), 0) == iota((n, n), 1)


def to_col(row):
    n = row.shape[1]
    return jnp.sum(jnp.where(eye_mask(n), row, 0.0), axis=1, keepdims=True)


def gram(rows):
    high, low = split(rows)
    left = jnp.concatenate([high, high, low], axis=0)
    return mm(left, jnp.concatenate([high, low, high], axis=0), TN)


def full_sum(value):
    return jnp.sum(jnp.sum(value, axis=1, keepdims=True), axis=0, keepdims=True)


def kernel(
    dims,
    feat_in,
    kern,
    gain,
    bias,
    mix_in,
    cot_in,
    mixed_out,
    gfeat_out,
    gmix_out,
    ggain_out,
    gbias_out,
    gker_out,
    gwhite_out,
    feat,
    mix,
    cot,
    tall,
    kpad,
    kst,
    ktst,
    xpad,
    dpad,
    cot2,
    xedge,
    dedge,
    xrows,
    drows,
    xside,
    dside,
    conv,
    dact,
    act,
    dnorm,
    gacc,
    bacc,
    kgrad,
    order,
    between,
    mrow,
    msend,
    mrecv,
    mcsend,
    mcrecv,
    send1,
    recv1,
    csend1,
    crecv1,
    cov,
    send2,
    recv2,
    csend2,
    crecv2,
    white,
    send3,
    recv3,
    csend3,
    crecv3,
    gmix,
    send4,
    recv4,
    csend4,
    crecv4,
    gker,
    in_sems,
    hsems,
    rs_s,
    rs_r,
    cx_s,
    cx_r,
    ag_s,
    ag_r,
    mr_s,
    mr_r,
    mc_s,
    mc_r,
):
    ndp, nrow, ncol, height, width = dims
    chans = feat_in.shape[0]
    gwidth = chans // GROUPS
    cells = height * width
    total = cells * nrow * ncol
    chunk = chans // nrow
    nwide = ndp * ncol
    block = 2 * width
    nblk = cells // block
    edge_rows = 2 * height
    middle = slice(width, width + cells)
    dp = lax.axis_index("dp")
    row = lax.axis_index("row")
    col = lax.axis_index("col")

    side = math.isqrt(nrow)
    ys = [lax.rem(row // side + step, side) for step in range(side)]
    xs = [lax.rem(lax.rem(row, side) + step, side) for step in range(side)]
    cs = [lax.rem(col + step, ncol) for step in range(ncol)]
    dps = [lax.rem(dp + step, ndp) for step in range(ndp)]

    def far(*offsets):
        return -sum(min(step, count - step) for step, count in offsets)

    row_order = sorted(
        ((y, x) for y in range(side) for x in range(side) if y + x > 0),
        key=lambda at: far((at[0], side), (at[1], side)),
    )
    wide_order = sorted(
        ((d, c) for d in range(ndp) for c in range(ncol) if d + c > 0),
        key=lambda at: far((at[1], ncol)),
    )
    col_order = [at for at in wide_order if at[0] == 0]
    row_to = [ys[y] * side + xs[x] for y, x in row_order]
    row_from = [ys[-y % side] * side + xs[-x % side] for y, x in row_order]

    def row_peer(k):
        return (dp, row_to[k], col)

    def col_peer(k):
        return (dp, row, cs[col_order[k][1]])

    def col_from(k):
        return cs[-col_order[k][1] % ncol]

    def wide_peer(k):
        return (dps[wide_order[k][0]], row, cs[wide_order[k][1]])

    def wide_from(k):
        return dps[-wide_order[k][0] % ndp] * ncol + cs[-wide_order[k][1] % ncol]

    def side_peer(step):
        return (
            dp,
            lax.rem(row + step[0] + nrow, nrow),
            lax.rem(col + step[1] + ncol, ncol),
        )

    loads = [
        pltpu.make_async_copy(source, target, in_sems.at[i])
        for i, (source, target) in enumerate(((feat_in, feat), (mix_in, mix), (cot_in, cot)))
    ]
    for load in loads:
        load.start()
    barrier = pltpu.get_barrier_semaphore()

    def greet(peer):
        pl.semaphore_signal(barrier, inc=1, device_id=peer, device_id_type=MESH)

    for k in range(nrow - 1):
        greet(row_peer(k))
    for k in range(nwide - 1):
        greet(wide_peer(k))

    for step in SIDES[2:]:
        greet(side_peer(step))

    lane = iota((chans, width), 1)

    def put(pad, tile, value):
        lanes = pl.ds(pl.multiple_of(tile * width, width), width)
        pad[1, :, lanes] = value.astype(BF16)
        pad[0, :, lanes] = jnp.where(lane == 0, 0.0, pltpu.roll(value, 1, 1)).astype(BF16)
        pad[2, :, lanes] = jnp.where(
            lane == width - 1, 0.0, pltpu.roll(value, width - 1, 1)
        ).astype(BF16)

    def edges(source, edge):
        index = iota((edge_rows, cells), 0)
        cell = jnp.where(index < height, index * width, (index - height) * width + width - 1)
        chosen = (iota((edge_rows, cells), 1) == cell).astype(F32).astype(BF16)
        edge[...] = mm(chosen, source[1, :, middle], NT).astype(BF16)

    def halo_copies(source, edge, rows, sides, base):
        copies = []
        for slot, (step, lanes) in enumerate(
            (((1, 0), pl.ds(cells, width)), ((-1, 0), pl.ds(width, width)))
        ):
            copies.append(
                pltpu.make_async_remote_copy(
                    src_ref=source.at[1, :, lanes],
                    dst_ref=rows.at[slot],
                    send_sem=hsems.at[base + slot],
                    recv_sem=hsems.at[base + 8 + slot],
                    device_id=side_peer(step),
                    device_id_type=MESH,
                )
            )
        for slot, step in enumerate(SIDES):
            copies.append(
                pltpu.make_async_remote_copy(
                    src_ref=edge,
                    dst_ref=sides.at[slot],
                    send_sem=hsems.at[base + 2 + slot],
                    recv_sem=hsems.at[base + 10 + slot],
                    device_id=side_peer((-step[0], -step[1])),
                    device_id_type=MESH,
                )
            )
        return copies

    has_up, has_down = row > 0, row < nrow - 1
    has_left, has_right = col > 0, col < ncol - 1

    def patch(rows, sides, pad):
        side = sides[...].astype(F32).reshape(8 * edge_rows, chans).T
        at = iota((chans, 8 * edge_rows), 1) // edge_rows
        for slot, step in enumerate(SIDES):
            live = has_left if step[1] < 0 else has_right
            if step[0] < 0:
                live = jnp.logical_and(live, has_up)
            if step[0] > 0:
                live = jnp.logical_and(live, has_down)
            side = jnp.where(at == jnp.where(live, -1, slot), 0.0, side)

        def bring(slot, line, left):
            index = slot * edge_rows + line + (height if left else 0)
            shift = (0 if left else width - 1) - index
            return pltpu.roll(side, shift % (8 * edge_rows), 1)[:, :width]

        for tile, which, left, right, line, live in (
            (0, 0, 2, 3, height - 1, has_up),
            (height + 1, 1, 4, 5, 0, has_down),
        ):
            value = rows[which].astype(F32)
            value = jnp.where(live, value, 0.0)
            lanes = slice(tile * width, (tile + 1) * width)
            pad[1, :, lanes] = value.astype(BF16)
            pad[0, :, lanes] = jnp.where(
                lane == 0, bring(left, line, True), pltpu.roll(value, 1, 1)
            ).astype(BF16)
            pad[2, :, lanes] = jnp.where(
                lane == width - 1, bring(right, line, False), pltpu.roll(value, width - 1, 1)
            ).astype(BF16)
        for line in range(height):
            lanes = slice((line + 1) * width, (line + 2) * width)
            pad[0, :, lanes] = jnp.where(
                lane == 0, bring(0, line, True), pad[0, :, lanes].astype(F32)
            ).astype(BF16)
            pad[2, :, lanes] = jnp.where(
                lane == width - 1, bring(1, line, False), pad[2, :, lanes].astype(F32)
            ).astype(BF16)

    def window(pad, tap, start, size):
        shift_row, shift_col = divmod(tap, 3)
        return pad[shift_col, :, pl.ds(pl.multiple_of(start + shift_row * width, width), size)]

    def line_of(index):
        return pl.ds(index, chans, stride=height)

    loads[0].wait()
    tall[...] = feat[...].astype(F32).reshape(chans * height, width)
    for r in range(height):
        put(xpad, r + 1, tall[line_of(r), :])
    edges(xpad, xedge)
    pl.semaphore_wait(barrier, (nrow - 1) + (nwide - 1) + 4)
    halo1 = halo_copies(xpad, xedge, xrows, xside, 0)
    for copy in halo1:
        copy.start()

    kpad[...] = jnp.zeros_like(kpad)
    kpad[: 9 * gwidth] = kern[...]
    own_group = (iota((chans, chans), 0) // gwidth) == (iota((chans, chans), 1) // gwidth)

    def pick(tap):
        tapcol = iota((128, chans), 0)
        within = lax.rem(iota((128, chans), 1), gwidth)
        return (tapcol == 9 * within + tap).astype(F32).astype(BF16)

    @pl.loop(0, 9)
    def _(tap):
        dense = jnp.where(own_group, mm(kpad[...], pick(tap), TN), 0.0)
        kst[:, pl.ds(pl.multiple_of(tap * chans, chans), chans)] = dense.astype(BF16)
        other = jnp.where(own_group, mm(pick(tap), kpad[...], TN), 0.0)
        ktst[:, pl.ds(pl.multiple_of((8 - tap) * chans, chans), chans)] = other.astype(BF16)

    conv[chans:] = jnp.ones((128, cells), BF16)
    loads[1].wait()
    loads[2].wait()
    tall[...] = cot[...].astype(F32).reshape(chans * height, width)
    for r in range(height):
        cot2[:, r * width : (r + 1) * width] = tall[line_of(r), :].astype(BF16)

    @pl.loop(0, nblk)
    def _(n):
        lanes = pl.ds(pl.multiple_of(n * block, block), block)
        dact[:, lanes] = mm(mix[...], cot2[:, lanes], TN)

    for copy in halo1:
        copy.wait_recv()

    patch(xrows, xside, xpad)

    @pl.loop(0, nblk)
    def _(n):
        lanes = pl.ds(pl.multiple_of(n * block, block), block)
        taps = [window(xpad, tap, n * block, block) for tap in range(9)]
        conv[:chans, lanes] = mm(kst[...], jnp.concatenate(taps, axis=0)).astype(BF16)

    def scatter(red, send, recv, k):
        return pltpu.make_async_remote_copy(
            src_ref=send.at[row_to[k]],
            dst_ref=recv.at[k],
            send_sem=rs_s.at[red, k],
            recv_sem=rs_r.at[red, k],
            device_id=row_peer(k),
            device_id_type=MESH,
        )

    def scatter_send(red, send, recv):
        for k in range(nrow - 1):
            scatter(red, send, recv, k).start()
        recv[nrow - 1] = send[row]

    def scatter_start(red, send, recv, full):
        send[...] = full.astype(BF16).reshape(send.shape)
        scatter_send(red, send, recv)

    def ordered_sum(slots):
        value = slots[0].astype(F32)
        for j in range(1, slots.shape[0]):
            value = value + slots[j].astype(F32)
        return value

    def scatter_wait(red, send, recv):
        for k in range(nrow - 1):
            scatter(red, send, recv, k).wait_recv()
        return ordered_sum(recv)

    def exchange(red, csend, crecv, wide, k, slot):
        return pltpu.make_async_remote_copy(
            src_ref=csend,
            dst_ref=crecv.at[slot],
            send_sem=cx_s.at[red, k],
            recv_sem=cx_r.at[red, k],
            device_id=wide_peer(k) if wide else col_peer(k),
            device_id_type=MESH,
        )

    def exchange_start(red, csend, crecv, wide, value):
        mine = dp * ncol + col if wide else col
        csend[...] = value.astype(BF16)
        for k in range(crecv.shape[0] - 1):
            exchange(red, csend, crecv, wide, k, mine).start()
        crecv[mine] = value.astype(BF16)

    def exchange_wait(red, csend, crecv, wide):
        for k in range(crecv.shape[0] - 1):
            source = wide_from(k) if wide else col_from(k)
            exchange(red, csend, crecv, wide, k, source).wait_recv()
        return ordered_sum(crecv)

    def gather(red, full, k, owner):
        rows = pl.ds(pl.multiple_of(owner * chunk, chunk), chunk)
        return pltpu.make_async_remote_copy(
            src_ref=full.at[rows],
            dst_ref=full.at[rows],
            send_sem=ag_s.at[red, k],
            recv_sem=ag_r.at[red, k],
            device_id=row_peer(k),
            device_id_type=MESH,
        )

    def gather_start(red, full, value):
        full[pl.ds(pl.multiple_of(row * chunk, chunk), chunk)] = value.astype(BF16)
        for k in range(nrow - 1):
            gather(red, full, k, row).start()

    def gather_wait(red, full):
        for k in range(nrow - 1):
            gather(red, full, k, row_from[k]).wait_recv()

    def spread(red, over_row, k, slot):
        return pltpu.make_async_remote_copy(
            src_ref=(msend if over_row else mcsend).at[red],
            dst_ref=(mrecv if over_row else mcrecv).at[red, slot],
            send_sem=(mr_s if over_row else mc_s).at[red, k],
            recv_sem=(mr_r if over_row else mc_r).at[red, k],
            device_id=row_peer(k) if over_row else col_peer(k),
            device_id_type=MESH,
        )

    def spread_start(red, over_row, value):
        mine = row if over_row else col
        (msend if over_row else mcsend)[red] = value
        for k in range((nrow if over_row else ncol) - 1):
            spread(red, over_row, k, mine).start()
        (mrecv if over_row else mcrecv)[red, mine] = value

    def spread_wait(red, over_row):
        count = nrow if over_row else ncol
        for k in range(count - 1):
            spread(red, over_row, k, row_from[k] if over_row else col_from(k)).wait_recv()
        for j in range(count):
            mrow[j : j + 1] = (mrecv if over_row else mcrecv)[red, j]
        return mrow[:count]

    def row_sums(source):
        return mm(jnp.ones((16, cells), BF16), source, NT)[:1]

    def centred(source, line):
        both = mm(source, conv[...], NT)
        sums = jnp.concatenate([both[:, chans:]] * (chans // 128), axis=1)
        return both[:, :chans] - sums * line

    local_mean = row_sums(conv[:chans]) * (1.0 / cells)
    spread_start(0, True, local_mean)
    scatter_start(0, send1, recv1, centred(conv[:chans], local_mean))
    plane = spread_wait(0, True)
    plane_mean = jnp.sum(plane, axis=0, keepdims=True) * (1.0 / nrow)
    spread_start(0, False, plane_mean)
    between[...] = gram(plane - plane_mean) * float(cells)
    mine = pl.ds(pl.multiple_of(row * chunk, chunk), chunk)
    partial = scatter_wait(0, send1, recv1) + between[mine]
    exchange_start(0, csend1, crecv1, False, partial)
    gather_start(0, cov, exchange_wait(0, csend1, crecv1, False))
    planes = spread_wait(0, False)
    mean = jnp.sum(planes, axis=0, keepdims=True) * (1.0 / ncol)
    diag = eye_mask(chans)
    between[...] = gram(planes - mean) * float(cells * nrow)
    gain_col = to_col(gain[...])
    bias_col = to_col(bias[...])
    gather_wait(0, cov)

    covariance = (cov[...].astype(F32) + between[...]) * (1.0 / total) + jnp.where(diag, EPS, 0.0)
    trace = full_sum(jnp.where(diag, covariance, 0.0))
    inv_trace = 1.0 / trace
    inv_root = lax.rsqrt(trace)
    normal = covariance * inv_trace
    normal2 = mm3(normal, normal)
    projs = [jnp.where(diag, 1.5, 0.0) - 0.5 * normal]
    squares = [jnp.where(diag, 2.25, 0.0) - 1.5 * normal + 0.25 * normal2]
    mixes = [1.5 * normal - 0.5 * normal2]
    for k in range(1, NEWTON):
        if k > 1:
            squares.append(mm3(projs[-1], projs[-1]))
            mixes.append(mm3(projs[-1], normal))
        projs.append(1.5 * projs[-1] - 0.5 * mm3(squares[-1], mixes[-1]))
    whiten = projs[-1] * inv_root
    wmean = jnp.sum(whiten * mean, axis=1, keepdims=True)
    whigh, wlow = split(whiten)
    wpair = jnp.concatenate([whigh, wlow], axis=1)

    gacc[...] = jnp.zeros_like(gacc)
    bacc[...] = jnp.zeros_like(bacc)

    @pl.loop(0, nblk)
    def _(n):
        lanes = pl.ds(pl.multiple_of(n * block, block), block)
        here = conv[:chans, lanes]
        normed = mm(wpair, jnp.concatenate([here, here], axis=0)) - wmean
        shifted = gain_col * normed + bias_col
        gate = jax.nn.sigmoid(shifted)
        act[:, lanes] = (shifted * gate).astype(BF16)
        dshift = dact[:, lanes] * gate * (1.0 + shifted * (1.0 - gate))
        dnorm[:, lanes] = (gain_col * dshift).astype(BF16)
        weighted = dshift * normed
        gacc[...] += weighted[:, :width] + weighted[:, width:]
        bacc[...] += dshift[:, :width] + dshift[:, width:]

    scatter_start(1, send2, recv2, centred(dnorm[...], mean))
    spread_start(1, True, row_sums(dnorm[...]))

    for n in range(nblk):
        for half in range(2):
            r = 2 * n + half
            added = mm(mix[...], act[:, r * width : (r + 1) * width])
            added = added + xpad[1, :, (r + 1) * width : (r + 2) * width].astype(F32)
            tall[line_of(r), :] = added

    spread_start(1, False, jnp.sum(spread_wait(1, True), axis=0, keepdims=True))
    exchange_start(1, csend2, crecv2, False, scatter_wait(1, send2, recv2))
    mixed_out[...] = tall[...].reshape(chans, height, width).astype(BF16)
    send3[...] = mm(cot2[...], act[...], NT).astype(BF16).reshape(send3.shape)
    grad_sum = jnp.sum(spread_wait(1, False), axis=0, keepdims=True)
    gather_start(1, white, exchange_wait(1, csend2, crecv2, False))
    wsum = jnp.sum(whiten * grad_sum, axis=1, keepdims=True) * (1.0 / total)
    gain_sum = jnp.sum(gacc[...], axis=1, keepdims=True)
    bias_sum = jnp.sum(bacc[...], axis=1, keepdims=True)
    gather_wait(1, white)
    scatter_send(2, send3, recv3)

    dwhiten = white[...].astype(F32)
    gwhite_out[...] = dwhiten * (1.0 / float(total) ** 0.5)
    sym = 0.5 * (dwhiten + dwhiten.T)
    cross = mm3(sym, normal)
    dproj = -0.5 * sym
    for k in range(NEWTON - 1):
        if k == 0:
            dsquare = -0.75 * sym + 0.25 * cross
            dmix = 1.5 * sym - 0.5 * (cross + cross.T)
        else:
            dsquare = mm3(dproj, projs[k])
            dmix = mm3(dproj, normal) + mm3(projs[k], sym)
        dsquare = dsquare + dsquare.T
        dproj = 1.5 * dproj - 0.5 * (mm3(dsquare, mixes[k]) + mm3(squares[k], dmix))

    scalar = full_sum(sym * projs[-1]) * 0.5 + full_sum(dproj * normal)
    dsym = inv_trace * inv_root * (dproj - jnp.where(diag, scalar, 0.0))
    dsym = (dsym + dsym.T) * (1.0 / total)
    exchange_start(2, csend3, crecv3, True, scatter_wait(2, send3, recv3))

    shift_col = wsum + jnp.sum(dsym * mean, axis=1, keepdims=True)
    dhigh, dlow = split(dsym)
    quad = jnp.concatenate([whigh, wlow, dhigh, dlow], axis=1)

    @pl.loop(0, nblk)
    def _(n):
        lanes = pl.ds(pl.multiple_of(n * block, block), block)
        one, two = dnorm[:, lanes], conv[:chans, lanes]
        value = mm(quad, jnp.concatenate([one, one, two, two], axis=0)) - shift_col
        put(dpad, 2 * n + 1, value[:, :width])
        put(dpad, 2 * n + 2, value[:, width:])

    edges(dpad, dedge)
    halo2 = halo_copies(dpad, dedge, drows, dside, 16)
    for copy in halo2:
        copy.start()

    turned = dpad[1, :, middle].T

    for tap in range(9):
        dense = mm(window(xpad, tap, 0, cells), turned)
        dense = jnp.where(own_group, dense, 0.0).reshape(GROUPS, gwidth, chans)
        kgrad[tap * gwidth : (tap + 1) * gwidth] = jnp.sum(dense, axis=0)

    kgrad[9 * gwidth :] = jnp.zeros((128 - 9 * gwidth, chans), F32)
    slim = iota((chans, 128), 1)
    grads = jnp.where(slim == 9 * gwidth, gain_sum, kgrad[...].T)
    grads = jnp.where(slim == 9 * gwidth + 1, bias_sum, grads)
    scatter_start(3, send4, recv4, grads)
    scale = 1.0 / float(ndp * total) ** 0.5
    for copy in halo2:
        copy.wait_recv()
    patch(drows, dside, dpad)
    exchange_start(3, csend4, crecv4, True, scatter_wait(3, send4, recv4))
    gather_start(2, gmix, exchange_wait(2, csend3, crecv3, True) * scale)

    def back(n):
        lanes = pl.ds(pl.multiple_of(n * block, block), block)
        taps = [window(dpad, tap, n * block, block) for tap in range(9)]
        value = mm(ktst[...], jnp.concatenate(taps, axis=0)) + cot2[:, lanes].astype(F32)
        tall[line_of(2 * n), :] = value[:, :width]
        tall[line_of(2 * n + 1), :] = value[:, width:]

    @pl.loop(0, nblk)
    def _(n):
        back(n)

    gather_start(3, gker, exchange_wait(3, csend4, crecv4, True) * scale)

    gfeat_out[...] = tall[...].reshape(chans, height, width).astype(BF16)
    for copy in halo1 + halo2:
        copy.wait_send()
    everything = (
        (send1, recv1, csend1, crecv1, cov),
        (send2, recv2, csend2, crecv2, white),
        (send3, recv3, csend3, crecv3, gmix),
        (send4, recv4, csend4, crecv4, gker),
    )
    for red, (send, recv, csend, crecv, full) in enumerate(everything):
        for k in range(nrow - 1):
            scatter(red, send, recv, k).wait_send()
            if red < 3:
                gather(red, full, k, row).wait_send()
        for k in range(crecv.shape[0] - 1):
            exchange(red, csend, crecv, red > 1, k, 0).wait_send()
    for red in range(2):
        for k in range(nrow - 1):
            spread(red, True, k, 0).wait_send()
        for k in range(ncol - 1):
            spread(red, False, k, 0).wait_send()

    gather_wait(2, gmix)
    gmix_out[...] = gmix[...].astype(F32)
    gather_wait(3, gker)
    final = gker[...].astype(F32).T
    for half in range(chans // 128):
        lanes = slice(half * 128, (half + 1) * 128)
        for tap in range(9):
            lines = final[tap * gwidth : (tap + 1) * gwidth, lanes]
            order[half, pl.ds(tap, gwidth, stride=9), :] = lines
        gker_out[:, lanes] = order[half]
    ggain_out[...] = final[9 * gwidth : 9 * gwidth + 1]
    gbias_out[...] = final[9 * gwidth + 1 : 9 * gwidth + 2]
    for k in range(nrow - 1):
        gather(3, gker, k, row).wait_send()


def store(*refs):
    sems = refs[-1]
    count = len(refs) // 2
    copies = [
        pltpu.make_async_copy(refs[i], refs[count + i], sems.at[i]) for i in range(count)
    ]
    for copy in copies:
        copy.start()
    for copy in copies:
        copy.wait()


def solution(mesh):
    ndp, nrow, ncol = (mesh.shape[name] for name in ("dp", "row", "col"))

    def local(features, group_kernel, norm_gain, norm_bias, mix_weight, cotangent):
        chans, height, width = features.shape[1:]
        cells = height * width
        chunk = chans // nrow
        nwide = ndp * ncol
        padded = cells + 2 * width

        def reduction(cols, wide):
            return [
                pltpu.VMEM((nrow, chunk, cols), BF16),
                pltpu.VMEM((nrow, chunk, cols), BF16),
                pltpu.VMEM((chunk, cols), BF16),
                pltpu.VMEM((nwide if wide else ncol, chunk, cols), BF16),
                pltpu.VMEM((chans, cols), BF16),
            ]

        vmem = pl.BlockSpec(memory_space=pltpu.VMEM)
        anywhere = pl.BlockSpec(memory_space=pl.ANY)
        results = (
            ((chans, height, width), BF16),
            ((chans, height, width), BF16),
            ((chans, chans), F32),
            ((1, chans), F32),
            ((1, chans), F32),
            (group_kernel.shape[::-1], F32),
            ((chans, chans), F32),
        )
        outs = pl.pallas_call(
            functools.partial(kernel, (ndp, nrow, ncol, height, width)),
            out_shape=tuple(pltpu.VMEM(shape, dtype) for shape, dtype in results),
            in_specs=[anywhere, vmem, vmem, vmem, anywhere, anywhere],
            out_specs=[vmem] * 7,
            scratch_shapes=[
                pltpu.VMEM((chans, height, width), BF16),
                pltpu.VMEM((chans, chans), BF16),
                pltpu.VMEM((chans, height, width), BF16),
                pltpu.VMEM((chans * height, width), F32),
                pltpu.VMEM((128, chans), BF16),
                pltpu.VMEM((chans, 9 * chans), BF16),
                pltpu.VMEM((chans, 9 * chans), BF16),
                pltpu.VMEM((3, chans, padded), BF16),
                pltpu.VMEM((3, chans, padded), BF16),
                pltpu.VMEM((chans, cells), BF16),
                pltpu.VMEM((2 * height, chans), BF16),
                pltpu.VMEM((2 * height, chans), BF16),
                pltpu.VMEM((2, chans, width), BF16),
                pltpu.VMEM((2, chans, width), BF16),
                pltpu.VMEM((8, 2 * height, chans), BF16),
                pltpu.VMEM((8, 2 * height, chans), BF16),
                pltpu.VMEM((chans + 128, cells), BF16),
                pltpu.VMEM((chans, cells), F32),
                pltpu.VMEM((chans, cells), BF16),
                pltpu.VMEM((chans, cells), BF16),
                pltpu.VMEM((chans, 128), F32),
                pltpu.VMEM((chans, 128), F32),
                pltpu.VMEM((128, chans), F32),
                pltpu.VMEM((chans // 128, group_kernel.shape[1], 128), F32),
                pltpu.VMEM((chans, chans), F32),
                pltpu.VMEM((max(nrow, ncol), chans), F32),
                pltpu.VMEM((2, 1, chans), F32),
                pltpu.VMEM((2, nrow, 1, chans), F32),
                pltpu.VMEM((2, 1, chans), F32),
                pltpu.VMEM((2, ncol, 1, chans), F32),
                *reduction(chans, False),
                *reduction(chans, False),
                *reduction(chans, True),
                *reduction(128, True),
                pltpu.SemaphoreType.DMA((3,)),
                pltpu.SemaphoreType.DMA((32,)),
                pltpu.SemaphoreType.DMA((4, nrow)),
                pltpu.SemaphoreType.DMA((4, nrow)),
                pltpu.SemaphoreType.DMA((4, nwide)),
                pltpu.SemaphoreType.DMA((4, nwide)),
                pltpu.SemaphoreType.DMA((4, nrow)),
                pltpu.SemaphoreType.DMA((4, nrow)),
                pltpu.SemaphoreType.DMA((2, nrow)),
                pltpu.SemaphoreType.DMA((2, nrow)),
                pltpu.SemaphoreType.DMA((2, ncol)),
                pltpu.SemaphoreType.DMA((2, ncol)),
            ],
            compiler_params=pltpu.CompilerParams(
                collective_id=0, has_side_effects=True, vmem_limit_bytes=60 * 1024 * 1024
            ),
        )(
            features.reshape(chans, height, width),
            group_kernel.T,
            norm_gain.reshape(1, chans),
            norm_bias.reshape(1, chans),
            mix_weight,
            cotangent.reshape(chans, height, width),
        )
        mixed, gfeat, gmix, ggain, gbias, gker, gwhite = pl.pallas_call(
            store,
            out_shape=tuple(jax.ShapeDtypeStruct(shape, dtype) for shape, dtype in results),
            in_specs=[anywhere] * 7,
            out_specs=[anywhere] * 7,
            scratch_shapes=[pltpu.SemaphoreType.DMA((7,))],
        )(*(pltpu.with_memory_space_constraint(out, pltpu.VMEM) for out in outs))
        return (
            mixed.reshape(features.shape),
            gfeat.reshape(features.shape),
            gmix,
            ggain.reshape(chans),
            gbias.reshape(chans),
            gker.T,
            gwhite[None],
        )

    in_specs = (P("dp", None, "row", "col"), P(), P(), P(), P(), P("dp", None, "row", "col"))
    out_specs = (
        P("dp", None, "row", "col"),
        P("dp", None, "row", "col"),
        P(),
        P(),
        P(),
        P(),
        P("dp", None, None),
    )
    return jax.shard_map(local, mesh=mesh, in_specs=in_specs, out_specs=out_specs, check_vma=False)
```

```python
import functools
import math

import jax
import jax.numpy as jnp
from jax import lax
from jax.experimental import pallas as pl
from jax.experimental.pallas import tpu as pltpu
from jax.sharding import PartitionSpec as P

GROUPS = 32
NEWTON = 5
EPS = 1e-05
MESH = pl.DeviceIdType.MESH
F32 = jnp.float32
BF16 = jnp.bfloat16

NN = (((1,), (0,)), ((), ()))
NT = (((1,), (1,)), ((), ()))
TN = (((0,), (0,)), ((), ()))

SIDES = ((0, -1), (0, 1), (-1, -1), (-1, 1), (1, -1), (1, 1))


def mm(a, b, dims=NN):
    return lax.dot_general(a, b, dims, preferred_element_type=F32)


def split(a):
    high = a.astype(BF16)
    return high, (a - high.astype(F32)).astype(BF16)


def mm3(a, b):
    ah, al = split(a)
    bh, bl = split(b)
    return mm(jnp.concatenate([ah, ah, al], axis=1), jnp.concatenate([bh, bl, bh], axis=0))


def iota(shape, dim):
    return lax.broadcasted_iota(jnp.int32, shape, dim)


def eye_mask(n):
    return iota((n, n), 0) == iota((n, n), 1)


def to_col(row):
    n = row.shape[1]
    return jnp.sum(jnp.where(eye_mask(n), row, 0.0), axis=1, keepdims=True)


def gram(rows):
    high, low = split(rows)
    left = jnp.concatenate([high, high, low], axis=0)
    return mm(left, jnp.concatenate([high, low, high], axis=0), TN)


def full_sum(value):
    return jnp.sum(jnp.sum(value, axis=1, keepdims=True), axis=0, keepdims=True)


def kernel(
    dims,
    feat_in,
    kern_in,
    gain_in,
    bias_in,
    mix_in,
    cot_in,
    mixed_out,
    gfeat_out,
    gmix_out,
    ggain_out,
    gbias_out,
    gker_out,
    gwhite_out,
    feat,
    mix,
    cot,
    kern,
    gain,
    bias,
    tall,
    kpad,
    kst,
    ktst,
    xpad,
    dpad,
    cot2,
    xedge,
    dedge,
    xrows,
    drows,
    xside,
    dside,
    conv,
    dact,
    act,
    dnorm,
    gacc,
    bacc,
    kgrad,
    order,
    between,
    mrow,
    msend,
    mrecv,
    mcsend,
    mcrecv,
    send1,
    recv1,
    csend1,
    crecv1,
    cov,
    send2,
    recv2,
    csend2,
    crecv2,
    white,
    send3,
    recv3,
    csend3,
    crecv3,
    gmix,
    send4,
    recv4,
    csend4,
    crecv4,
    gker,
    in_sems,
    hsems,
    rs_s,
    rs_r,
    cx_s,
    cx_r,
    ag_s,
    ag_r,
    mr_s,
    mr_r,
    mc_s,
    mc_r,
):
    ndp, nrow, ncol, height, width = dims
    chans = feat_in.shape[0]
    gwidth = chans // GROUPS
    cells = height * width
    total = cells * nrow * ncol
    chunk = chans // nrow
    nwide = ndp * ncol
    block = 2 * width
    nblk = cells // block
    edge_rows = 2 * height
    middle = slice(width, width + cells)
    dp = lax.axis_index("dp")
    row = lax.axis_index("row")
    col = lax.axis_index("col")

    side = math.isqrt(nrow)
    ys = [lax.rem(row // side + step, side) for step in range(side)]
    xs = [lax.rem(lax.rem(row, side) + step, side) for step in range(side)]
    cs = [lax.rem(col + step, ncol) for step in range(ncol)]
    dps = [lax.rem(dp + step, ndp) for step in range(ndp)]

    def far(*offsets):
        return -sum(min(step, count - step) for step, count in offsets)

    row_order = sorted(
        ((y, x) for y in range(side) for x in range(side) if y + x > 0),
        key=lambda at: far((at[0], side), (at[1], side)),
    )
    wide_order = sorted(
        ((d, c) for d in range(ndp) for c in range(ncol) if d + c > 0),
        key=lambda at: far((at[1], ncol)),
    )
    col_order = [at for at in wide_order if at[0] == 0]
    row_to = [ys[y] * side + xs[x] for y, x in row_order]

    def row_peer(k):
        return (dp, row_to[k], col)

    def col_peer(k):
        return (dp, row, cs[col_order[k][1]])

    def wide_peer(k):
        return (dps[wide_order[k][0]], row, cs[wide_order[k][1]])

    def side_peer(step):
        return (
            dp,
            lax.rem(row + step[0] + nrow, nrow),
            lax.rem(col + step[1] + ncol, ncol),
        )

    arguments = (
        (feat_in, feat),
        (mix_in, mix),
        (cot_in, cot),
        (kern_in, kern),
        (gain_in, gain),
        (bias_in, bias),
    )
    loads = [
        pltpu.make_async_copy(source, target, in_sems.at[i])
        for i, (source, target) in enumerate(arguments)
    ]
    for load in loads:
        load.start()
    def whole(ref, count, send_sem, recv_sem):
        part = ref.at[pl.ds(0, count)]
        return pltpu.make_async_remote_copy(
            src_ref=part,
            dst_ref=part,
            send_sem=send_sem,
            recv_sem=recv_sem,
            device_id=row_peer(0),
            device_id_type=MESH,
        )

    barrier = pltpu.get_barrier_semaphore()

    def greet(peer):
        pl.semaphore_signal(barrier, inc=1, device_id=peer, device_id_type=MESH)

    for k in range(nrow - 1):
        greet(row_peer(k))
    for k in range(nwide - 1):
        greet(wide_peer(k))

    for step in SIDES[2:]:
        greet(side_peer(step))

    lane = iota((chans, width), 1)

    def put(pad, tile, value):
        lanes = pl.ds(pl.multiple_of(tile * width, width), width)
        pad[1, :, lanes] = value.astype(BF16)
        pad[0, :, lanes] = jnp.where(lane == 0, 0.0, pltpu.roll(value, 1, 1)).astype(BF16)
        pad[2, :, lanes] = jnp.where(
            lane == width - 1, 0.0, pltpu.roll(value, width - 1, 1)
        ).astype(BF16)

    def edges(source, edge):
        index = iota((edge_rows, cells), 0)
        cell = jnp.where(index < height, index * width, (index - height) * width + width - 1)
        chosen = (iota((edge_rows, cells), 1) == cell).astype(F32).astype(BF16)
        edge[...] = mm(chosen, source[1, :, middle], NT).astype(BF16)

    def halo_copies(source, edge, rows, sides, base):
        copies = []
        for slot, (step, lanes) in enumerate(
            (((1, 0), pl.ds(cells, width)), ((-1, 0), pl.ds(width, width)))
        ):
            copies.append(
                pltpu.make_async_remote_copy(
                    src_ref=source.at[1, :, lanes],
                    dst_ref=rows.at[slot],
                    send_sem=hsems.at[base],
                    recv_sem=hsems.at[base + 1],
                    device_id=side_peer(step),
                    device_id_type=MESH,
                )
            )
        for slot, step in enumerate(SIDES):
            copies.append(
                pltpu.make_async_remote_copy(
                    src_ref=edge,
                    dst_ref=sides.at[slot],
                    send_sem=hsems.at[base + 2],
                    recv_sem=hsems.at[base + 3],
                    device_id=side_peer((-step[0], -step[1])),
                    device_id_type=MESH,
                )
            )
        for copy in copies:
            copy.start()

    def halo_waits(rows, sides, base):
        return (
            whole(rows, 2, hsems.at[base], hsems.at[base + 1]),
            whole(sides, len(SIDES), hsems.at[base + 2], hsems.at[base + 3]),
        )

    has_up, has_down = row > 0, row < nrow - 1
    has_left, has_right = col > 0, col < ncol - 1

    def patch(rows, sides, pad, fresh):
        side = sides[...].astype(F32).reshape(8 * edge_rows, chans).T
        at = iota((chans, 8 * edge_rows), 1) // edge_rows
        for slot, step in enumerate(SIDES):
            live = has_left if step[1] < 0 else has_right
            if step[0] < 0:
                live = jnp.logical_and(live, has_up)
            if step[0] > 0:
                live = jnp.logical_and(live, has_down)
            side = jnp.where(at == jnp.where(live, -1, slot), 0.0, side)

        def bring(slot, line, left):
            index = slot * edge_rows + line + (height if left else 0)
            shift = (0 if left else width - 1) - index
            return pltpu.roll(side, shift % (8 * edge_rows), 1)[:, :width]

        for tile, which, left, right, line, live in (
            (0, 0, 2, 3, height - 1, has_up),
            (height + 1, 1, 4, 5, 0, has_down),
        ):
            value = rows[which].astype(F32)
            value = jnp.where(live, value, 0.0)
            lanes = slice(tile * width, (tile + 1) * width)
            pad[1, :, lanes] = value.astype(BF16)
            pad[0, :, lanes] = jnp.where(
                lane == 0, bring(left, line, True), pltpu.roll(value, 1, 1)
            ).astype(BF16)
            pad[2, :, lanes] = jnp.where(
                lane == width - 1, bring(right, line, False), pltpu.roll(value, width - 1, 1)
            ).astype(BF16)
        for line in range(height):
            lanes = slice((line + 1) * width, (line + 2) * width)
            if fresh:
                value = pad[1, :, lanes].astype(F32)
                before, after = pltpu.roll(value, 1, 1), pltpu.roll(value, width - 1, 1)
            else:
                before, after = pad[0, :, lanes].astype(F32), pad[2, :, lanes].astype(F32)
            pad[0, :, lanes] = jnp.where(lane == 0, bring(0, line, True), before).astype(BF16)
            pad[2, :, lanes] = jnp.where(
                lane == width - 1, bring(1, line, False), after
            ).astype(BF16)

    def window(pad, tap, start, size):
        shift_row, shift_col = divmod(tap, 3)
        return pad[shift_col, :, pl.ds(pl.multiple_of(start + shift_row * width, width), size)]

    def line_of(index):
        return pl.ds(index, chans, stride=height)

    loads[0].wait()
    tall[...] = feat[...].astype(F32).reshape(chans * height, width)
    for r in range(height):
        put(xpad, r + 1, tall[line_of(r), :])
    edges(xpad, xedge)
    pl.semaphore_wait(barrier, (nrow - 1) + (nwide - 1) + 4)
    halo_copies(xpad, xedge, xrows, xside, 0)

    for load in loads[3:]:
        load.wait()
    kpad[...] = jnp.zeros_like(kpad)
    kpad[: 9 * gwidth] = kern[...]
    own_group = (iota((chans, chans), 0) // gwidth) == (iota((chans, chans), 1) // gwidth)

    def pick(tap):
        tapcol = iota((128, chans), 0)
        within = lax.rem(iota((128, chans), 1), gwidth)
        return (tapcol == 9 * within + tap).astype(F32).astype(BF16)

    @pl.loop(0, 9)
    def _(tap):
        dense = jnp.where(own_group, mm(kpad[...], pick(tap), TN), 0.0)
        kst[:, pl.ds(pl.multiple_of(tap * chans, chans), chans)] = dense.astype(BF16)
        other = jnp.where(own_group, mm(pick(tap), kpad[...], TN), 0.0)
        ktst[:, pl.ds(pl.multiple_of((8 - tap) * chans, chans), chans)] = other.astype(BF16)

    conv[chans:] = jnp.ones((128, cells), BF16)
    loads[1].wait()
    loads[2].wait()
    tall[...] = cot[...].astype(F32).reshape(chans * height, width)
    for r in range(height):
        cot2[:, r * width : (r + 1) * width] = tall[line_of(r), :].astype(BF16)

    @pl.loop(0, nblk)
    def _(n):
        lanes = pl.ds(pl.multiple_of(n * block, block), block)
        dact[:, lanes] = mm(mix[...], cot2[:, lanes], TN)

    for wait in halo_waits(xrows, xside, 0):
        wait.wait_recv()

    patch(xrows, xside, xpad, False)

    @pl.loop(0, nblk)
    def _(n):
        lanes = pl.ds(pl.multiple_of(n * block, block), block)
        taps = [window(xpad, tap, n * block, block) for tap in range(9)]
        conv[:chans, lanes] = mm(kst[...], jnp.concatenate(taps, axis=0)).astype(BF16)

    def all_scattered(red, recv):
        return whole(recv, nrow - 1, rs_s.at[red], rs_r.at[red])

    def all_exchanged(red, crecv):
        return whole(crecv, crecv.shape[0] - 1, cx_s.at[red], cx_r.at[red])

    def all_gathered(red, full):
        return whole(full, chans - chunk, ag_s.at[red], ag_r.at[red])

    def all_spread(red, over_row):
        if over_row:
            return whole(mrecv.at[red], nrow - 1, mr_s.at[red], mr_r.at[red])
        return whole(mcrecv.at[red], ncol - 1, mc_s.at[red], mc_r.at[red])

    def scatter(red, send, recv, k):
        return pltpu.make_async_remote_copy(
            src_ref=send.at[row_to[k]],
            dst_ref=recv.at[k],
            send_sem=rs_s.at[red],
            recv_sem=rs_r.at[red],
            device_id=row_peer(k),
            device_id_type=MESH,
        )

    def scatter_send(red, send, recv):
        for k in range(nrow - 1):
            scatter(red, send, recv, k).start()
        recv[nrow - 1] = send[row]

    def scatter_start(red, send, recv, full):
        send[...] = full.astype(BF16).reshape(send.shape)
        scatter_send(red, send, recv)

    def ordered_sum(slots):
        value = slots[0].astype(F32)
        for j in range(1, slots.shape[0]):
            value = value + slots[j].astype(F32)
        return value

    def scatter_wait(red, send, recv):
        all_scattered(red, recv).wait_recv()
        return ordered_sum(recv)

    def exchange(red, csend, crecv, wide, k, slot):
        return pltpu.make_async_remote_copy(
            src_ref=csend,
            dst_ref=crecv.at[slot],
            send_sem=cx_s.at[red],
            recv_sem=cx_r.at[red],
            device_id=wide_peer(k) if wide else col_peer(k),
            device_id_type=MESH,
        )

    def exchange_start(red, csend, crecv, wide, value):
        mine = dp * ncol + col if wide else col
        csend[...] = value.astype(BF16)
        for k in range(crecv.shape[0] - 1):
            exchange(red, csend, crecv, wide, k, mine).start()
        crecv[mine] = value.astype(BF16)

    def exchange_wait(red, csend, crecv, wide):
        all_exchanged(red, crecv).wait_recv()
        return ordered_sum(crecv)

    def gather(red, full, k, owner):
        rows = pl.ds(pl.multiple_of(owner * chunk, chunk), chunk)
        return pltpu.make_async_remote_copy(
            src_ref=full.at[rows],
            dst_ref=full.at[rows],
            send_sem=ag_s.at[red],
            recv_sem=ag_r.at[red],
            device_id=row_peer(k),
            device_id_type=MESH,
        )

    def gather_start(red, full, value):
        full[pl.ds(pl.multiple_of(row * chunk, chunk), chunk)] = value.astype(BF16)
        for k in range(nrow - 1):
            gather(red, full, k, row).start()

    def gather_wait(red, full):
        all_gathered(red, full).wait_recv()

    def spread(red, over_row, k, slot):
        return pltpu.make_async_remote_copy(
            src_ref=(msend if over_row else mcsend).at[red],
            dst_ref=(mrecv if over_row else mcrecv).at[red, slot],
            send_sem=(mr_s if over_row else mc_s).at[red],
            recv_sem=(mr_r if over_row else mc_r).at[red],
            device_id=row_peer(k) if over_row else col_peer(k),
            device_id_type=MESH,
        )

    def spread_start(red, over_row, value):
        mine = row if over_row else col
        (msend if over_row else mcsend)[red] = value
        for k in range((nrow if over_row else ncol) - 1):
            spread(red, over_row, k, mine).start()
        (mrecv if over_row else mcrecv)[red, mine] = value

    def spread_wait(red, over_row):
        count = nrow if over_row else ncol
        all_spread(red, over_row).wait_recv()
        for j in range(count):
            mrow[j : j + 1] = (mrecv if over_row else mcrecv)[red, j]
        return mrow[:count]

    def row_sums(source):
        return mm(jnp.ones((16, cells), BF16), source, NT)[:1]

    def centred(both, line):
        sums = jnp.concatenate([both[:, chans:]] * (chans // 128), axis=1)
        return both[:, :chans] - sums * line

    local_mean = row_sums(conv[:chans]) * (1.0 / cells)
    spread_start(0, True, local_mean)
    scatter_start(0, send1, recv1, centred(mm(conv[:chans], conv[...], NT), local_mean))
    plane = spread_wait(0, True)
    plane_mean = jnp.sum(plane, axis=0, keepdims=True) * (1.0 / nrow)
    spread_start(0, False, plane_mean)
    between[...] = gram(plane - plane_mean) * float(cells)
    mine = pl.ds(pl.multiple_of(row * chunk, chunk), chunk)
    partial = scatter_wait(0, send1, recv1) + between[mine]
    exchange_start(0, csend1, crecv1, False, partial)
    gather_start(0, cov, exchange_wait(0, csend1, crecv1, False))
    planes = spread_wait(0, False)
    mean = jnp.sum(planes, axis=0, keepdims=True) * (1.0 / ncol)
    diag = eye_mask(chans)
    between[...] = gram(planes - mean) * float(cells * nrow)
    gain_col = to_col(gain[...])
    bias_col = to_col(bias[...])
    gather_wait(0, cov)

    covariance = (cov[...].astype(F32) + between[...]) * (1.0 / total) + jnp.where(diag, EPS, 0.0)
    trace = full_sum(jnp.where(diag, covariance, 0.0))
    inv_trace = 1.0 / trace
    inv_root = lax.rsqrt(trace)
    normal = covariance * inv_trace
    normal2 = mm3(normal, normal)
    projs = [jnp.where(diag, 1.5, 0.0) - 0.5 * normal]
    squares = [jnp.where(diag, 2.25, 0.0) - 1.5 * normal + 0.25 * normal2]
    mixes = [1.5 * normal - 0.5 * normal2]
    for k in range(1, NEWTON):
        if k > 1:
            squares.append(mm3(projs[-1], projs[-1]))
            mixes.append(mm3(projs[-1], normal))
        projs.append(1.5 * projs[-1] - 0.5 * mm3(squares[-1], mixes[-1]))
    whiten = projs[-1] * inv_root
    wmean = jnp.sum(whiten * mean, axis=1, keepdims=True)
    whigh, wlow = split(whiten)
    wpair = jnp.concatenate([whigh, wlow], axis=1)

    gain_part, bias_part, product = 0.0, 0.0, 0.0
    for n in range(nblk):
        lanes = slice(n * block, (n + 1) * block)
        here = conv[:chans, lanes]
        normed = mm(wpair, jnp.concatenate([here, here], axis=0)) - wmean
        shifted = gain_col * normed + bias_col
        gate = jax.nn.sigmoid(shifted)
        act[:, lanes] = (shifted * gate).astype(BF16)
        dshift = dact[:, lanes] * gate * (1.0 + shifted * (1.0 - gate))
        grads = (gain_col * dshift).astype(BF16)
        dnorm[:, lanes] = grads
        product = product + mm(grads, conv[:, lanes], NT)
        weighted = dshift * normed
        gain_part = gain_part + weighted[:, :width] + weighted[:, width:]
        bias_part = bias_part + dshift[:, :width] + dshift[:, width:]
    gacc[...] = gain_part
    bacc[...] = bias_part

    scatter_start(1, send2, recv2, centred(product, mean))
    spread_start(1, True, row_sums(dnorm[...]))

    for n in range(nblk):
        for half in range(2):
            r = 2 * n + half
            added = mm(mix[...], act[:, r * width : (r + 1) * width])
            added = added + xpad[1, :, (r + 1) * width : (r + 2) * width].astype(F32)
            tall[line_of(r), :] = added

    spread_start(1, False, jnp.sum(spread_wait(1, True), axis=0, keepdims=True))
    exchange_start(1, csend2, crecv2, False, scatter_wait(1, send2, recv2))
    mixed_out[...] = tall[...].reshape(chans, height, width).astype(BF16)
    send3[...] = mm(cot2[...], act[...], NT).astype(BF16).reshape(send3.shape)
    grad_sum = jnp.sum(spread_wait(1, False), axis=0, keepdims=True)
    gather_start(1, white, exchange_wait(1, csend2, crecv2, False))
    wsum = jnp.sum(whiten * grad_sum, axis=1, keepdims=True) * (1.0 / total)
    gain_sum = jnp.sum(gacc[...], axis=1, keepdims=True)
    bias_sum = jnp.sum(bacc[...], axis=1, keepdims=True)
    gather_wait(1, white)
    scatter_send(2, send3, recv3)

    dwhiten = white[...].astype(F32)
    gwhite_out[...] = dwhiten * (1.0 / float(total) ** 0.5)
    sym = 0.5 * (dwhiten + dwhiten.T)
    cross = mm3(sym, normal)
    dproj = -0.5 * sym
    for k in range(NEWTON - 1):
        if k == 0:
            dsquare = -0.75 * sym + 0.25 * cross
            dmix = 1.5 * sym - 0.5 * (cross + cross.T)
        else:
            dsquare = mm3(dproj, projs[k])
            dmix = mm3(dproj, normal) + mm3(projs[k], sym)
        dsquare = dsquare + dsquare.T
        dproj = 1.5 * dproj - 0.5 * (mm3(dsquare, mixes[k]) + mm3(squares[k], dmix))

    scalar = full_sum(sym * projs[-1]) * 0.5 + full_sum(dproj * normal)
    dsym = inv_trace * inv_root * (dproj - jnp.where(diag, scalar, 0.0))
    dsym = (dsym + dsym.T) * (1.0 / total)
    exchange_start(2, csend3, crecv3, True, scatter_wait(2, send3, recv3))

    shift_col = wsum + jnp.sum(dsym * mean, axis=1, keepdims=True)
    dhigh, dlow = split(dsym)
    quad = jnp.concatenate([whigh, wlow, dhigh, dlow], axis=1)

    @pl.loop(0, nblk)
    def _(n):
        lanes = pl.ds(pl.multiple_of(n * block, block), block)
        one, two = dnorm[:, lanes], conv[:chans, lanes]
        value = mm(quad, jnp.concatenate([one, one, two, two], axis=0)) - shift_col
        dpad[1, :, pl.ds(pl.multiple_of(n * block + width, width), block)] = value.astype(BF16)

    turned = dpad[1, :, middle].T

    for tap in range(9):
        dense = mm(window(xpad, tap, 0, cells), turned)
        dense = jnp.where(own_group, dense, 0.0).reshape(GROUPS, gwidth, chans)
        kgrad[tap * gwidth : (tap + 1) * gwidth] = jnp.sum(dense, axis=0)

    kgrad[9 * gwidth :] = jnp.zeros((128 - 9 * gwidth, chans), F32)
    slim = iota((chans, 128), 1)
    grads = jnp.where(slim == 9 * gwidth, gain_sum, kgrad[...].T)
    grads = jnp.where(slim == 9 * gwidth + 1, bias_sum, grads)
    scatter_start(3, send4, recv4, grads)
    scale = 1.0 / float(ndp * total) ** 0.5
    edges(dpad, dedge)
    halo_copies(dpad, dedge, drows, dside, 4)
    exchange_start(3, csend4, crecv4, True, scatter_wait(3, send4, recv4))
    gather_start(2, gmix, exchange_wait(2, csend3, crecv3, True) * scale)
    for wait in halo_waits(drows, dside, 4):
        wait.wait_recv()
    patch(drows, dside, dpad, True)

    def back(n):
        lanes = pl.ds(pl.multiple_of(n * block, block), block)
        taps = [window(dpad, tap, n * block, block) for tap in range(9)]
        value = mm(ktst[...], jnp.concatenate(taps, axis=0)) + cot2[:, lanes].astype(F32)
        tall[line_of(2 * n), :] = value[:, :width]
        tall[line_of(2 * n + 1), :] = value[:, width:]

    @pl.loop(0, nblk)
    def _(n):
        back(n)

    gather_start(3, gker, exchange_wait(3, csend4, crecv4, True) * scale)

    gfeat_out[...] = tall[...].reshape(chans, height, width).astype(BF16)
    for wait in halo_waits(xrows, xside, 0) + halo_waits(drows, dside, 4):
        wait.wait_send()
    everything = (
        (send1, recv1, csend1, crecv1, cov),
        (send2, recv2, csend2, crecv2, white),
        (send3, recv3, csend3, crecv3, gmix),
        (send4, recv4, csend4, crecv4, gker),
    )
    for red, (send, recv, csend, crecv, full) in enumerate(everything):
        all_scattered(red, recv).wait_send()
        all_exchanged(red, crecv).wait_send()
        if red < 3:
            all_gathered(red, full).wait_send()
    for red in range(2):
        all_spread(red, True).wait_send()
        all_spread(red, False).wait_send()

    gather_wait(2, gmix)
    gmix_out[...] = gmix[...].astype(F32)
    gather_wait(3, gker)
    final = gker[...].astype(F32).T
    for half in range(chans // 128):
        lanes = slice(half * 128, (half + 1) * 128)
        for tap in range(9):
            lines = final[tap * gwidth : (tap + 1) * gwidth, lanes]
            order[half, pl.ds(tap, gwidth, stride=9), :] = lines
        gker_out[:, lanes] = order[half]
    ggain_out[...] = final[9 * gwidth : 9 * gwidth + 1]
    gbias_out[...] = final[9 * gwidth + 1 : 9 * gwidth + 2]
    all_gathered(3, gker).wait_send()


def store(*refs):
    sems = refs[-1]
    count = len(refs) // 2
    copies = [
        pltpu.make_async_copy(refs[i], refs[count + i], sems.at[i]) for i in range(count)
    ]
    for copy in copies:
        copy.start()
    for copy in copies:
        copy.wait()


def solution(mesh):
    ndp, nrow, ncol = (mesh.shape[name] for name in ("dp", "row", "col"))

    def local(features, group_kernel, norm_gain, norm_bias, mix_weight, cotangent):
        chans, height, width = features.shape[1:]
        cells = height * width
        chunk = chans // nrow
        nwide = ndp * ncol
        padded = cells + 2 * width

        def reduction(cols, wide):
            return [
                pltpu.VMEM((nrow, chunk, cols), BF16),
                pltpu.VMEM((nrow, chunk, cols), BF16),
                pltpu.VMEM((chunk, cols), BF16),
                pltpu.VMEM((nwide if wide else ncol, chunk, cols), BF16),
                pltpu.VMEM((chans, cols), BF16),
            ]

        vmem = pl.BlockSpec(memory_space=pltpu.VMEM)
        anywhere = pl.BlockSpec(memory_space=pl.ANY)
        results = (
            ((chans, height, width), BF16),
            ((chans, height, width), BF16),
            ((chans, chans), F32),
            ((1, chans), F32),
            ((1, chans), F32),
            (group_kernel.shape[::-1], F32),
            ((chans, chans), F32),
        )
        outs = pl.pallas_call(
            functools.partial(kernel, (ndp, nrow, ncol, height, width)),
            out_shape=tuple(pltpu.VMEM(shape, dtype) for shape, dtype in results),
            in_specs=[anywhere] * 6,
            out_specs=[vmem] * 7,
            scratch_shapes=[
                pltpu.VMEM((chans, height, width), BF16),
                pltpu.VMEM((chans, chans), BF16),
                pltpu.VMEM((chans, height, width), BF16),
                pltpu.VMEM(group_kernel.shape[::-1], BF16),
                pltpu.VMEM((1, chans), F32),
                pltpu.VMEM((1, chans), F32),
                pltpu.VMEM((chans * height, width), F32),
                pltpu.VMEM((128, chans), BF16),
                pltpu.VMEM((chans, 9 * chans), BF16),
                pltpu.VMEM((chans, 9 * chans), BF16),
                pltpu.VMEM((3, chans, padded), BF16),
                pltpu.VMEM((3, chans, padded), BF16),
                pltpu.VMEM((chans, cells), BF16),
                pltpu.VMEM((2 * height, chans), BF16),
                pltpu.VMEM((2 * height, chans), BF16),
                pltpu.VMEM((2, chans, width), BF16),
                pltpu.VMEM((2, chans, width), BF16),
                pltpu.VMEM((8, 2 * height, chans), BF16),
                pltpu.VMEM((8, 2 * height, chans), BF16),
                pltpu.VMEM((chans + 128, cells), BF16),
                pltpu.VMEM((chans, cells), F32),
                pltpu.VMEM((chans, cells), BF16),
                pltpu.VMEM((chans, cells), BF16),
                pltpu.VMEM((chans, 128), F32),
                pltpu.VMEM((chans, 128), F32),
                pltpu.VMEM((128, chans), F32),
                pltpu.VMEM((chans // 128, group_kernel.shape[1], 128), F32),
                pltpu.VMEM((chans, chans), F32),
                pltpu.VMEM((max(nrow, ncol), chans), F32),
                pltpu.VMEM((2, 1, chans), F32),
                pltpu.VMEM((2, nrow, 1, chans), F32),
                pltpu.VMEM((2, 1, chans), F32),
                pltpu.VMEM((2, ncol, 1, chans), F32),
                *reduction(chans, False),
                *reduction(chans, False),
                *reduction(chans, True),
                *reduction(128, True),
                pltpu.SemaphoreType.DMA((6,)),
                pltpu.SemaphoreType.DMA((8,)),
                *[pltpu.SemaphoreType.DMA((4,))] * 6,
                *[pltpu.SemaphoreType.DMA((2,))] * 4,
            ],
            compiler_params=pltpu.CompilerParams(
                collective_id=0, has_side_effects=True, vmem_limit_bytes=60 * 1024 * 1024
            ),
        )(
            features.reshape(chans, height, width),
            group_kernel.T,
            norm_gain.reshape(1, chans),
            norm_bias.reshape(1, chans),
            mix_weight,
            cotangent.reshape(chans, height, width),
        )
        mixed, gfeat, gmix, ggain, gbias, gker, gwhite = pl.pallas_call(
            store,
            out_shape=tuple(jax.ShapeDtypeStruct(shape, dtype) for shape, dtype in results),
            in_specs=[anywhere] * 7,
            out_specs=[anywhere] * 7,
            scratch_shapes=[pltpu.SemaphoreType.DMA((7,))],
        )(*(pltpu.with_memory_space_constraint(out, pltpu.VMEM) for out in outs))
        return (
            mixed.reshape(features.shape),
            gfeat.reshape(features.shape),
            gmix,
            ggain.reshape(chans),
            gbias.reshape(chans),
            gker.T,
            gwhite[None],
        )

    in_specs = (P("dp", None, "row", "col"), P(), P(), P(), P(), P("dp", None, "row", "col"))
    out_specs = (
        P("dp", None, "row", "col"),
        P("dp", None, "row", "col"),
        P(),
        P(),
        P(),
        P(),
        P("dp", None, None),
    )
    return jax.shard_map(local, mesh=mesh, in_specs=in_specs, out_specs=out_specs, check_vma=False)
```

```python
import functools
import math

import jax
import jax.numpy as jnp
from jax import lax
from jax.experimental import pallas as pl
from jax.experimental.pallas import tpu as pltpu
from jax.sharding import PartitionSpec as P

GROUPS = 32
NEWTON = 5
EPS = 1e-05
MESH = pl.DeviceIdType.MESH
F32 = jnp.float32
BF16 = jnp.bfloat16

NN = (((1,), (0,)), ((), ()))
NT = (((1,), (1,)), ((), ()))
TN = (((0,), (0,)), ((), ()))

SIDES = ((0, -1), (0, 1), (-1, -1), (-1, 1), (1, -1), (1, 1))


def mm(a, b, dims=NN):
    return lax.dot_general(a, b, dims, preferred_element_type=F32)


def split(a):
    high = a.astype(BF16)
    return high, (a - high.astype(F32)).astype(BF16)


def left(a):
    high, low = split(a)
    return jnp.concatenate([high, high, low], axis=1)


def right(b):
    high, low = split(b)
    return jnp.concatenate([high, low, high], axis=0)


def iota(shape, dim):
    return lax.broadcasted_iota(jnp.int32, shape, dim)


def eye_mask(n):
    return iota((n, n), 0) == iota((n, n), 1)


def to_col(row):
    n = row.shape[1]
    return jnp.sum(jnp.where(eye_mask(n), row, 0.0), axis=1, keepdims=True)


def gram(rows):
    high, low = split(rows)
    left = jnp.concatenate([high, high, low], axis=0)
    return mm(left, jnp.concatenate([high, low, high], axis=0), TN)


def full_sum(value):
    return jnp.sum(jnp.sum(value, axis=1, keepdims=True), axis=0, keepdims=True)


def kernel(
    dims,
    feat_in,
    kern_in,
    gain_in,
    bias_in,
    mix_in,
    cot_in,
    mixed_out,
    gfeat_out,
    gmix_out,
    ggain_out,
    gbias_out,
    gker_out,
    gwhite_out,
    feat,
    mix,
    cot,
    kern,
    gain,
    bias,
    tall,
    kpad,
    kst,
    ktst,
    xpad,
    dpad,
    cot2,
    xedge,
    dedge,
    xrows,
    drows,
    xside,
    dside,
    conv,
    alone,
    dact,
    act,
    dnorm,
    gacc,
    bacc,
    kgrad,
    order,
    between,
    mrow,
    mplane,
    mblock,
    msend,
    mrecv,
    mcsend,
    mcrecv,
    send1,
    recv1,
    csend1,
    crecv1,
    cov,
    send2,
    recv2,
    csend2,
    crecv2,
    white,
    send3,
    recv3,
    csend3,
    crecv3,
    gmix,
    send4,
    recv4,
    csend4,
    crecv4,
    gker,
    in_sems,
    hsems,
    rs_s,
    rs_r,
    cx_s,
    cx_r,
    ag_s,
    ag_r,
    mr_s,
    mr_r,
    mc_s,
    mc_r,
):
    ndp, nrow, ncol, height, width = dims
    chans = feat_in.shape[0]
    gwidth = chans // GROUPS
    cells = height * width
    total = cells * nrow * ncol
    chunk = chans // nrow
    nwide = ndp * ncol
    block = 2 * width
    nblk = cells // block
    edge_rows = 2 * height
    middle = slice(width, width + cells)
    dp = lax.axis_index("dp")
    row = lax.axis_index("row")
    col = lax.axis_index("col")

    side = math.isqrt(nrow)
    ys = [lax.rem(row // side + step, side) for step in range(side)]
    xs = [lax.rem(lax.rem(row, side) + step, side) for step in range(side)]
    cs = [lax.rem(col + step, ncol) for step in range(ncol)]
    dps = [lax.rem(dp + step, ndp) for step in range(ndp)]

    def far(*offsets):
        return -sum(min(step, count - step) for step, count in offsets)

    row_order = sorted(
        ((y, x) for y in range(side) for x in range(side) if y + x > 0),
        key=lambda at: far((at[0], side), (at[1], side)),
    )
    wide_order = sorted(
        ((d, c) for d in range(ndp) for c in range(ncol) if d + c > 0),
        key=lambda at: far((at[1], ncol)),
    )
    col_order = [at for at in wide_order if at[0] == 0]
    row_to = [ys[y] * side + xs[x] for y, x in row_order]

    def row_peer(k):
        return (dp, row_to[k], col)

    def col_peer(k):
        return (dp, row, cs[col_order[k][1]])

    def wide_peer(k):
        return (dps[wide_order[k][0]], row, cs[wide_order[k][1]])

    def side_peer(step):
        return (
            dp,
            lax.rem(row + step[0] + nrow, nrow),
            lax.rem(col + step[1] + ncol, ncol),
        )

    arguments = (
        (feat_in, feat),
        (mix_in, mix),
        (cot_in, cot),
        (kern_in, kern),
        (gain_in, gain),
        (bias_in, bias),
    )
    loads = [
        pltpu.make_async_copy(source, target, in_sems.at[i])
        for i, (source, target) in enumerate(arguments)
    ]
    for load in loads:
        load.start()
    def whole(ref, count, send_sem, recv_sem):
        part = ref.at[pl.ds(0, count)]
        return pltpu.make_async_remote_copy(
            src_ref=part,
            dst_ref=part,
            send_sem=send_sem,
            recv_sem=recv_sem,
            device_id=row_peer(0),
            device_id_type=MESH,
        )

    barrier = pltpu.get_barrier_semaphore()

    def greet(peer):
        pl.semaphore_signal(barrier, inc=1, device_id=peer, device_id_type=MESH)

    for k in range(nrow - 1):
        greet(row_peer(k))
    for k in range(nwide - 1):
        greet(wide_peer(k))

    for step in SIDES[2:]:
        greet(side_peer(step))

    lane = iota((chans, width), 1)

    def put(pad, tile, value):
        lanes = pl.ds(pl.multiple_of(tile * width, width), width)
        pad[1, :, lanes] = value.astype(BF16)
        pad[0, :, lanes] = jnp.where(lane == 0, 0.0, pltpu.roll(value, 1, 1)).astype(BF16)
        pad[2, :, lanes] = jnp.where(
            lane == width - 1, 0.0, pltpu.roll(value, width - 1, 1)
        ).astype(BF16)

    def edges(source, edge):
        index = iota((edge_rows, cells), 0)
        cell = jnp.where(index < height, index * width, (index - height) * width + width - 1)
        chosen = (iota((edge_rows, cells), 1) == cell).astype(F32).astype(BF16)
        edge[...] = mm(chosen, source[1, :, middle], NT).astype(BF16)

    def halo_copies(source, edge, rows, sides, base):
        copies = []
        for slot, (step, lanes) in enumerate(
            (((1, 0), pl.ds(cells, width)), ((-1, 0), pl.ds(width, width)))
        ):
            copies.append(
                pltpu.make_async_remote_copy(
                    src_ref=source.at[1, :, lanes],
                    dst_ref=rows.at[slot],
                    send_sem=hsems.at[base],
                    recv_sem=hsems.at[base + 1],
                    device_id=side_peer(step),
                    device_id_type=MESH,
                )
            )
        for slot, step in enumerate(SIDES):
            copies.append(
                pltpu.make_async_remote_copy(
                    src_ref=edge,
                    dst_ref=sides.at[slot],
                    send_sem=hsems.at[base + 2],
                    recv_sem=hsems.at[base + 3],
                    device_id=side_peer((-step[0], -step[1])),
                    device_id_type=MESH,
                )
            )
        for copy in copies:
            copy.start()

    def halo_waits(rows, sides, base):
        return (
            whole(rows, 2, hsems.at[base], hsems.at[base + 1]),
            whole(sides, len(SIDES), hsems.at[base + 2], hsems.at[base + 3]),
        )

    has_up, has_down = row > 0, row < nrow - 1
    has_left, has_right = col > 0, col < ncol - 1

    def side_lanes(sides):
        side_map = sides[...].astype(F32).reshape(8 * edge_rows, chans).T
        at = iota((chans, 8 * edge_rows), 1) // edge_rows
        for slot, step in enumerate(SIDES):
            live = has_left if step[1] < 0 else has_right
            if step[0] < 0:
                live = jnp.logical_and(live, has_up)
            if step[0] > 0:
                live = jnp.logical_and(live, has_down)
            side_map = jnp.where(at == jnp.where(live, -1, slot), 0.0, side_map)
        return jnp.where(at < len(SIDES), side_map, 0.0)

    def bring(side_map, slot, line, first):
        index = slot * edge_rows + line + (height if first else 0)
        shift = (0 if first else width - 1) - index
        return pltpu.roll(side_map, shift % (8 * edge_rows), 1)[:, :width]

    def put_ends(rows, side_map, pad):
        for tile, which, before, after, line, live in (
            (0, 0, 2, 3, height - 1, has_up),
            (height + 1, 1, 4, 5, 0, has_down),
        ):
            value = jnp.where(live, rows[which].astype(F32), 0.0)
            lanes = slice(tile * width, (tile + 1) * width)
            pad[1, :, lanes] = value.astype(BF16)
            pad[0, :, lanes] = jnp.where(
                lane == 0, bring(side_map, before, line, True), pltpu.roll(value, 1, 1)
            ).astype(BF16)
            pad[2, :, lanes] = jnp.where(
                lane == width - 1,
                bring(side_map, after, line, False),
                pltpu.roll(value, width - 1, 1),
            ).astype(BF16)

    def put_columns(side_map, pad, fresh):
        for line in range(height):
            lanes = slice((line + 1) * width, (line + 2) * width)
            if fresh:
                value = pad[1, :, lanes].astype(F32)
                before, after = pltpu.roll(value, 1, 1), pltpu.roll(value, width - 1, 1)
            else:
                before, after = pad[0, :, lanes].astype(F32), pad[2, :, lanes].astype(F32)
            pad[0, :, lanes] = jnp.where(
                lane == 0, bring(side_map, 0, line, True), before
            ).astype(BF16)
            pad[2, :, lanes] = jnp.where(
                lane == width - 1, bring(side_map, 1, line, False), after
            ).astype(BF16)

    def window(pad, tap, start, size):
        shift_row, shift_col = divmod(tap, 3)
        return pad[shift_col, :, pl.ds(pl.multiple_of(start + shift_row * width, width), size)]

    def line_of(index):
        return pl.ds(index, chans, stride=height)

    loads[0].wait()
    tall[...] = feat[...].astype(F32).reshape(chans * height, width)
    for r in range(height):
        put(xpad, r + 1, tall[line_of(r), :])
    edges(xpad, xedge)
    loads[3].wait()
    kpad[...] = jnp.zeros_like(kpad)
    kpad[: 9 * gwidth] = kern[...]
    own_group = (iota((chans, chans), 0) // gwidth) == (iota((chans, chans), 1) // gwidth)

    def pick(tap):
        tapcol = iota((128, chans), 0)
        within = lax.rem(iota((128, chans), 1), gwidth)
        return (tapcol == 9 * within + tap).astype(F32).astype(BF16)

    @pl.loop(0, 9)
    def _(tap):
        dense = jnp.where(own_group, mm(kpad[...], pick(tap), TN), 0.0)
        kst[:, pl.ds(pl.multiple_of(tap * chans, chans), chans)] = dense.astype(BF16)

    for edge_tile in (slice(0, width), slice(width + cells, 2 * width + cells)):
        xpad[:, :, edge_tile] = jnp.zeros((3, chans, width), BF16)
    pl.semaphore_wait(barrier, (nrow - 1) + (nwide - 1) + 4)
    halo_copies(xpad, xedge, xrows, xside, 0)

    @pl.loop(0, nblk)
    def _(n):
        lanes = pl.ds(pl.multiple_of(n * block, block), block)
        taps = [window(xpad, tap, n * block, block) for tap in range(9)]
        alone[:, lanes] = mm(kst[...], jnp.concatenate(taps, axis=0))

    conv[chans:] = jnp.ones((128, cells), BF16)
    for wait in halo_waits(xrows, xside, 0):
        wait.wait_recv()

    side_map1 = side_lanes(xside)
    put_ends(xrows, side_map1, xpad)
    half = width // 2
    first_cols, last_cols = [], []
    for shift_row in range(3):
        for at, base, found in (
            (lane, height, first_cols),
            (lane - half, edge_rows - half, last_cols),
        ):
            source = at + shift_row - 1
            inside = jnp.logical_and(jnp.logical_and(at >= 0, at < height), source >= 0)
            inside = jnp.logical_and(inside, source < height)
            moved = pltpu.roll(side_map1, -(base + shift_row - 1) % width, 1)
            found.append(jnp.where(inside, moved, 0.0).astype(BF16))

    def weights(*taps):
        return jnp.concatenate([kst[:, tap * chans : (tap + 1) * chans] for tap in taps], axis=1)

    def end_rows(tile):
        lanes = slice(tile * width, (tile + 1) * width)
        return jnp.concatenate([xpad[which, :, lanes] for which in range(3)], axis=0)

    upper = mm(weights(0, 1, 2), end_rows(0))
    lower = mm(weights(6, 7, 8), end_rows(height + 1))
    columns = mm(weights(0, 3, 6, 2, 5, 8), jnp.concatenate(first_cols + last_cols, axis=0))
    for r in range(height):
        lanes = slice(r * width, (r + 1) * width)
        value = alone[:, lanes]
        if r == 0:
            value = value + upper
        if r == height - 1:
            value = value + lower
        value = value + jnp.where(lane == 0, pltpu.roll(columns, -r % width, 1), 0.0)
        value = value + jnp.where(
            lane == width - 1, pltpu.roll(columns, (half - 1 - r) % width, 1), 0.0
        )
        conv[:chans, lanes] = value.astype(BF16)

    def all_scattered(red, recv):
        return whole(recv, nrow - 1, rs_s.at[red], rs_r.at[red])

    def all_exchanged(red, crecv):
        return whole(crecv, crecv.shape[0] - 1, cx_s.at[red], cx_r.at[red])

    def all_gathered(red, full):
        return whole(full, chans - chunk, ag_s.at[red], ag_r.at[red])

    def all_spread(red, over_row):
        if over_row:
            return whole(mrecv.at[red], nrow - 1, mr_s.at[red], mr_r.at[red])
        return whole(mcrecv.at[red], ncol - 1, mc_s.at[red], mc_r.at[red])

    def scatter(red, send, recv, k):
        return pltpu.make_async_remote_copy(
            src_ref=send.at[row_to[k]],
            dst_ref=recv.at[k],
            send_sem=rs_s.at[red],
            recv_sem=rs_r.at[red],
            device_id=row_peer(k),
            device_id_type=MESH,
        )

    def scatter_send(red, send, recv):
        for k in range(nrow - 1):
            scatter(red, send, recv, k).start()
        recv[nrow - 1] = send[row]

    def scatter_start(red, send, recv, full):
        send[...] = full.astype(BF16).reshape(send.shape)
        scatter_send(red, send, recv)

    def ordered_sum(slots):
        value = slots[0].astype(F32)
        for j in range(1, slots.shape[0]):
            value = value + slots[j].astype(F32)
        return value

    def scatter_wait(red, send, recv):
        all_scattered(red, recv).wait_recv()
        return ordered_sum(recv)

    def exchange(red, csend, crecv, wide, k, slot):
        return pltpu.make_async_remote_copy(
            src_ref=csend,
            dst_ref=crecv.at[slot],
            send_sem=cx_s.at[red],
            recv_sem=cx_r.at[red],
            device_id=wide_peer(k) if wide else col_peer(k),
            device_id_type=MESH,
        )

    def exchange_start(red, csend, crecv, wide, value):
        mine = dp * ncol + col if wide else col
        csend[...] = value.astype(BF16)
        for k in range(crecv.shape[0] - 1):
            exchange(red, csend, crecv, wide, k, mine).start()
        crecv[mine] = value.astype(BF16)

    def exchange_wait(red, csend, crecv, wide):
        all_exchanged(red, crecv).wait_recv()
        return ordered_sum(crecv)

    def gather(red, full, k, owner):
        rows = pl.ds(pl.multiple_of(owner * chunk, chunk), chunk)
        return pltpu.make_async_remote_copy(
            src_ref=full.at[rows],
            dst_ref=full.at[rows],
            send_sem=ag_s.at[red],
            recv_sem=ag_r.at[red],
            device_id=row_peer(k),
            device_id_type=MESH,
        )

    def gather_start(red, full, value):
        full[pl.ds(pl.multiple_of(row * chunk, chunk), chunk)] = value.astype(BF16)
        for k in range(nrow - 1):
            gather(red, full, k, row).start()

    def gather_wait(red, full):
        all_gathered(red, full).wait_recv()

    def spread(red, over_row, k, slot):
        return pltpu.make_async_remote_copy(
            src_ref=(msend if over_row else mcsend).at[red],
            dst_ref=(mrecv if over_row else mcrecv).at[red, slot],
            send_sem=(mr_s if over_row else mc_s).at[red],
            recv_sem=(mr_r if over_row else mc_r).at[red],
            device_id=row_peer(k) if over_row else col_peer(k),
            device_id_type=MESH,
        )

    def spread_start(red, over_row, value):
        mine = row if over_row else col
        (msend if over_row else mcsend)[red] = value
        for k in range((nrow if over_row else ncol) - 1):
            spread(red, over_row, k, mine).start()
        (mrecv if over_row else mcrecv)[red, mine] = value

    def spread_wait(red, over_row):
        count = nrow if over_row else ncol
        all_spread(red, over_row).wait_recv()
        for j in range(count):
            mrow[j : j + 1] = (mrecv if over_row else mcrecv)[red, j]
        return mrow[:count]

    def planes_copy(k, slot):
        return pltpu.make_async_remote_copy(
            src_ref=mplane,
            dst_ref=mblock.at[slot],
            send_sem=mc_s.at[0],
            recv_sem=mc_r.at[0],
            device_id=col_peer(k),
            device_id_type=MESH,
        )

    def row_sums(source):
        return mm(jnp.ones((16, cells), BF16), source, NT)[:1]

    def centred(both, line):
        sums = jnp.concatenate([both[:, chans:]] * (chans // 128), axis=1)
        return both[:, :chans] - sums * line

    raw = mm(conv[: chans + 16], conv[...], NT)
    local_mean = raw[chans : chans + 1, :chans] * (1.0 / cells)
    scatter_start(0, send1, recv1, centred(raw[:chans], local_mean))
    spread_start(0, True, local_mean)
    for load in loads[4:]:
        load.wait()

    @pl.loop(0, 9)
    def _(tap):
        other = jnp.where(own_group, mm(pick(tap), kpad[...], TN), 0.0)
        ktst[:, pl.ds(pl.multiple_of((8 - tap) * chans, chans), chans)] = other.astype(BF16)

    loads[1].wait()
    loads[2].wait()
    tall[...] = cot[...].astype(F32).reshape(chans * height, width)
    for r in range(height):
        cot2[:, r * width : (r + 1) * width] = tall[line_of(r), :].astype(BF16)

    exchange_start(0, csend1, crecv1, False, scatter_wait(0, send1, recv1))
    mplane[...] = spread_wait(0, True)
    for k in range(ncol - 1):
        planes_copy(k, col).start()
    mblock[col] = mplane[...]
    gather_start(0, cov, exchange_wait(0, csend1, crecv1, False))
    whole(mblock, ncol - 1, mc_s.at[0], mc_r.at[0]).wait_recv()
    means = mblock[...].reshape(nrow * ncol, chans)
    mean = jnp.sum(means, axis=0, keepdims=True) * (1.0 / (nrow * ncol))
    between[...] = gram(means - mean) * float(cells)
    diag = eye_mask(chans)
    gain_col = to_col(gain[...])
    bias_col = to_col(bias[...])
    put_columns(side_map1, xpad, False)

    @pl.loop(0, nblk)
    def _(n):
        lanes = pl.ds(pl.multiple_of(n * block, block), block)
        dact[:, lanes] = mm(mix[...], cot2[:, lanes], TN)

    gather_wait(0, cov)

    covariance = (cov[...].astype(F32) + between[...]) * (1.0 / total) + jnp.where(diag, EPS, 0.0)
    trace = full_sum(jnp.where(diag, covariance, 0.0))
    inv_trace = 1.0 / trace
    inv_root = lax.rsqrt(trace)
    normal = covariance * inv_trace
    normal_r = right(normal)
    normal2 = mm(left(normal), normal_r)
    projs = [jnp.where(diag, 1.5, 0.0) - 0.5 * normal]
    squares = [left(jnp.where(diag, 2.25, 0.0) - 1.5 * normal + 0.25 * normal2)]
    mixes = [right(1.5 * normal - 0.5 * normal2)]
    projs_l, projs_r = [None], [None]
    for k in range(1, NEWTON):
        if k > 1:
            projs_l.append(left(projs[-1]))
            projs_r.append(right(projs[-1]))
            both = mm(projs_l[-1], jnp.concatenate([projs_r[-1], normal_r], axis=1))
            squares.append(left(both[:, :chans]))
            mixes.append(right(both[:, chans:]))
        projs.append(1.5 * projs[-1] - 0.5 * mm(squares[-1], mixes[-1]))
    whiten = projs[-1] * inv_root
    wmean = jnp.sum(whiten * mean, axis=1, keepdims=True)
    whigh, wlow = split(whiten)
    wpair = jnp.concatenate([whigh, wlow], axis=1)

    gain_part, bias_part, product = 0.0, 0.0, 0.0
    for n in range(nblk):
        lanes = slice(n * block, (n + 1) * block)
        here = conv[:chans, lanes]
        normed = mm(wpair, jnp.concatenate([here, here], axis=0)) - wmean
        shifted = gain_col * normed + bias_col
        gate = jax.nn.sigmoid(shifted)
        act[:, lanes] = (shifted * gate).astype(BF16)
        dshift = dact[:, lanes] * gate * (1.0 + shifted * (1.0 - gate))
        grads = (gain_col * dshift).astype(BF16)
        dnorm[:, lanes] = grads
        product = product + mm(grads, conv[:, lanes], NT)
        weighted = dshift * normed
        gain_part = gain_part + weighted[:, :width] + weighted[:, width:]
        bias_part = bias_part + dshift[:, :width] + dshift[:, width:]
    gacc[...] = gain_part
    bacc[...] = bias_part

    scatter_start(1, send2, recv2, centred(product, mean))
    spread_start(1, True, row_sums(dnorm[...]))

    for n in range(nblk):
        for half in range(2):
            r = 2 * n + half
            added = mm(mix[...], act[:, r * width : (r + 1) * width])
            added = added + xpad[1, :, (r + 1) * width : (r + 2) * width].astype(F32)
            tall[line_of(r), :] = added

    exchange_start(1, csend2, crecv2, False, scatter_wait(1, send2, recv2))
    spread_start(1, False, jnp.sum(spread_wait(1, True), axis=0, keepdims=True))
    mixed_out[...] = tall[...].reshape(chans, height, width).astype(BF16)
    send3[...] = mm(cot2[...], act[...], NT).astype(BF16).reshape(send3.shape)
    gather_start(1, white, exchange_wait(1, csend2, crecv2, False))
    grad_sum = jnp.sum(spread_wait(1, False), axis=0, keepdims=True)
    wsum = jnp.sum(whiten * grad_sum, axis=1, keepdims=True) * (1.0 / total)
    gain_sum = jnp.sum(gacc[...], axis=1, keepdims=True)
    bias_sum = jnp.sum(bacc[...], axis=1, keepdims=True)
    gather_wait(1, white)
    scatter_send(2, send3, recv3)

    dwhiten = white[...].astype(F32)
    gwhite_out[...] = dwhiten * (1.0 / float(total) ** 0.5)
    sym = 0.5 * (dwhiten + dwhiten.T)
    sym_r = right(sym)
    cross = mm(left(sym), normal_r)
    dproj = -0.5 * sym
    sym_products = mm(jnp.concatenate(projs_l[1:], axis=0), sym_r)
    for k in range(NEWTON - 1):
        if k == 0:
            dsquare = -0.75 * sym + 0.25 * cross
            dmix = 1.5 * sym - 0.5 * (cross + cross.T)
        else:
            both = mm(left(dproj), jnp.concatenate([projs_r[k], normal_r], axis=1))
            dsquare = both[:, :chans]
            dmix = both[:, chans:] + sym_products[(k - 1) * chans : k * chans]
        dsquare = dsquare + dsquare.T
        change = mm(
            jnp.concatenate([left(dsquare), squares[k]], axis=1),
            jnp.concatenate([mixes[k], right(dmix)], axis=0),
        )
        dproj = 1.5 * dproj - 0.5 * change

    scalar = full_sum(sym * projs[-1]) * 0.5 + full_sum(dproj * normal)
    dsym = inv_trace * inv_root * (dproj - jnp.where(diag, scalar, 0.0))
    dsym = (dsym + dsym.T) * (1.0 / total)
    shift_col = wsum + jnp.sum(dsym * mean, axis=1, keepdims=True)
    dhigh, dlow = split(dsym)
    quad = jnp.concatenate([whigh, wlow, dhigh, dlow], axis=1)

    for n in range(nblk):
        lanes = slice(n * block, (n + 1) * block)
        one, two = dnorm[:, lanes], conv[:chans, lanes]
        value = mm(quad, jnp.concatenate([one, one, two, two], axis=0)) - shift_col
        dpad[1, :, n * block + width : (n + 1) * block + width] = value.astype(BF16)

    turned = dpad[1, :, middle].T

    for tap in range(9):
        dense = mm(window(xpad, tap, 0, cells), turned)
        dense = jnp.where(own_group, dense, 0.0).reshape(GROUPS, gwidth, chans)
        kgrad[tap * gwidth : (tap + 1) * gwidth] = jnp.sum(dense, axis=0)

    kgrad[9 * gwidth :] = jnp.zeros((128 - 9 * gwidth, chans), F32)
    slim = iota((chans, 128), 1)
    grads = jnp.where(slim == 9 * gwidth, gain_sum, kgrad[...].T)
    grads = jnp.where(slim == 9 * gwidth + 1, bias_sum, grads)
    scatter_start(3, send4, recv4, grads)
    scale = 1.0 / float(ndp * total) ** 0.5
    edges(dpad, dedge)
    halo_copies(dpad, dedge, drows, dside, 4)
    exchange_start(2, csend3, crecv3, True, scatter_wait(2, send3, recv3))
    exchange_start(3, csend4, crecv4, True, scatter_wait(3, send4, recv4))
    for wait in halo_waits(drows, dside, 4):
        wait.wait_recv()
    side_map2 = side_lanes(dside)
    put_ends(drows, side_map2, dpad)
    put_columns(side_map2, dpad, True)

    gather_start(2, gmix, exchange_wait(2, csend3, crecv3, True) * scale)

    def back(n):
        lanes = pl.ds(pl.multiple_of(n * block, block), block)
        taps = [window(dpad, tap, n * block, block) for tap in range(9)]
        value = mm(ktst[...], jnp.concatenate(taps, axis=0)) + cot2[:, lanes].astype(F32)
        tall[line_of(2 * n), :] = value[:, :width]
        tall[line_of(2 * n + 1), :] = value[:, width:]

    @pl.loop(0, nblk)
    def _(n):
        back(n)

    gather_start(3, gker, exchange_wait(3, csend4, crecv4, True) * scale)

    gfeat_out[...] = tall[...].reshape(chans, height, width).astype(BF16)
    for wait in halo_waits(xrows, xside, 0) + halo_waits(drows, dside, 4):
        wait.wait_send()
    everything = (
        (send1, recv1, csend1, crecv1, cov),
        (send2, recv2, csend2, crecv2, white),
        (send3, recv3, csend3, crecv3, gmix),
        (send4, recv4, csend4, crecv4, gker),
    )
    for red, (send, recv, csend, crecv, full) in enumerate(everything):
        all_scattered(red, recv).wait_send()
        all_exchanged(red, crecv).wait_send()
        if red < 3:
            all_gathered(red, full).wait_send()
    all_spread(0, True).wait_send()
    all_spread(1, True).wait_send()
    all_spread(1, False).wait_send()
    whole(mblock, ncol - 1, mc_s.at[0], mc_r.at[0]).wait_send()

    gather_wait(2, gmix)
    gmix_out[...] = gmix[...].astype(F32)
    gather_wait(3, gker)
    final = gker[...].astype(F32).T
    for half in range(chans // 128):
        lanes = slice(half * 128, (half + 1) * 128)
        for tap in range(9):
            lines = final[tap * gwidth : (tap + 1) * gwidth, lanes]
            order[half, pl.ds(tap, gwidth, stride=9), :] = lines
        gker_out[:, lanes] = order[half]
    ggain_out[...] = final[9 * gwidth : 9 * gwidth + 1]
    gbias_out[...] = final[9 * gwidth + 1 : 9 * gwidth + 2]
    all_gathered(3, gker).wait_send()


def store(*refs):
    sems = refs[-1]
    count = len(refs) // 2
    copies = [
        pltpu.make_async_copy(refs[i], refs[count + i], sems.at[i]) for i in range(count)
    ]
    for copy in copies:
        copy.start()
    for copy in copies:
        copy.wait()


def solution(mesh):
    ndp, nrow, ncol = (mesh.shape[name] for name in ("dp", "row", "col"))

    def local(features, group_kernel, norm_gain, norm_bias, mix_weight, cotangent):
        chans, height, width = features.shape[1:]
        cells = height * width
        chunk = chans // nrow
        nwide = ndp * ncol
        padded = cells + 2 * width

        def reduction(cols, wide):
            return [
                pltpu.VMEM((nrow, chunk, cols), BF16),
                pltpu.VMEM((nrow, chunk, cols), BF16),
                pltpu.VMEM((chunk, cols), BF16),
                pltpu.VMEM((nwide if wide else ncol, chunk, cols), BF16),
                pltpu.VMEM((chans, cols), BF16),
            ]

        vmem = pl.BlockSpec(memory_space=pltpu.VMEM)
        anywhere = pl.BlockSpec(memory_space=pl.ANY)
        results = (
            ((chans, height, width), BF16),
            ((chans, height, width), BF16),
            ((chans, chans), F32),
            ((1, chans), F32),
            ((1, chans), F32),
            (group_kernel.shape[::-1], F32),
            ((chans, chans), F32),
        )
        outs = pl.pallas_call(
            functools.partial(kernel, (ndp, nrow, ncol, height, width)),
            out_shape=tuple(pltpu.VMEM(shape, dtype) for shape, dtype in results),
            in_specs=[anywhere] * 6,
            out_specs=[vmem] * 7,
            scratch_shapes=[
                pltpu.VMEM((chans, height, width), BF16),
                pltpu.VMEM((chans, chans), BF16),
                pltpu.VMEM((chans, height, width), BF16),
                pltpu.VMEM(group_kernel.shape[::-1], BF16),
                pltpu.VMEM((1, chans), F32),
                pltpu.VMEM((1, chans), F32),
                pltpu.VMEM((chans * height, width), F32),
                pltpu.VMEM((128, chans), BF16),
                pltpu.VMEM((chans, 9 * chans), BF16),
                pltpu.VMEM((chans, 9 * chans), BF16),
                pltpu.VMEM((3, chans, padded), BF16),
                pltpu.VMEM((3, chans, padded), BF16),
                pltpu.VMEM((chans, cells), BF16),
                pltpu.VMEM((2 * height, chans), BF16),
                pltpu.VMEM((2 * height, chans), BF16),
                pltpu.VMEM((2, chans, width), BF16),
                pltpu.VMEM((2, chans, width), BF16),
                pltpu.VMEM((8, 2 * height, chans), BF16),
                pltpu.VMEM((8, 2 * height, chans), BF16),
                pltpu.VMEM((chans + 128, cells), BF16),
                pltpu.VMEM((chans, cells), F32),
                pltpu.VMEM((chans, cells), F32),
                pltpu.VMEM((chans, cells), BF16),
                pltpu.VMEM((chans, cells), BF16),
                pltpu.VMEM((chans, 128), F32),
                pltpu.VMEM((chans, 128), F32),
                pltpu.VMEM((128, chans), F32),
                pltpu.VMEM((chans // 128, group_kernel.shape[1], 128), F32),
                pltpu.VMEM((chans, chans), F32),
                pltpu.VMEM((max(nrow, ncol), chans), F32),
                pltpu.VMEM((nrow, chans), F32),
                pltpu.VMEM((ncol, nrow, chans), F32),
                pltpu.VMEM((2, 1, chans), F32),
                pltpu.VMEM((2, nrow, 1, chans), F32),
                pltpu.VMEM((2, 1, chans), F32),
                pltpu.VMEM((2, ncol, 1, chans), F32),
                *reduction(chans, False),
                *reduction(chans, False),
                *reduction(chans, True),
                *reduction(128, True),
                pltpu.SemaphoreType.DMA((6,)),
                pltpu.SemaphoreType.DMA((8,)),
                *[pltpu.SemaphoreType.DMA((4,))] * 6,
                *[pltpu.SemaphoreType.DMA((2,))] * 4,
            ],
            compiler_params=pltpu.CompilerParams(
                collective_id=0, has_side_effects=True, vmem_limit_bytes=60 * 1024 * 1024
            ),
        )(
            features.reshape(chans, height, width),
            group_kernel.T,
            norm_gain.reshape(1, chans),
            norm_bias.reshape(1, chans),
            mix_weight,
            cotangent.reshape(chans, height, width),
        )
        mixed, gfeat, gmix, ggain, gbias, gker, gwhite = pl.pallas_call(
            store,
            out_shape=tuple(jax.ShapeDtypeStruct(shape, dtype) for shape, dtype in results),
            in_specs=[anywhere] * 7,
            out_specs=[anywhere] * 7,
            scratch_shapes=[pltpu.SemaphoreType.DMA((7,))],
        )(*(pltpu.with_memory_space_constraint(out, pltpu.VMEM) for out in outs))
        return (
            mixed.reshape(features.shape),
            gfeat.reshape(features.shape),
            gmix,
            ggain.reshape(chans),
            gbias.reshape(chans),
            gker.T,
            gwhite[None],
        )

    in_specs = (P("dp", None, "row", "col"), P(), P(), P(), P(), P("dp", None, "row", "col"))
    out_specs = (
        P("dp", None, "row", "col"),
        P("dp", None, "row", "col"),
        P(),
        P(),
        P(),
        P(),
        P("dp", None, None),
    )
    return jax.shard_map(local, mesh=mesh, in_specs=in_specs, out_specs=out_specs, check_vma=False)
```

```python
import functools
import math

import jax
import jax.numpy as jnp
from jax import lax
from jax.experimental import pallas as pl
from jax.experimental.pallas import tpu as pltpu
from jax.sharding import PartitionSpec as P

GROUPS = 32
NEWTON = 5
EPS = 1e-05
MESH = pl.DeviceIdType.MESH
F32 = jnp.float32
BF16 = jnp.bfloat16

NN = (((1,), (0,)), ((), ()))
NT = (((1,), (1,)), ((), ()))
TN = (((0,), (0,)), ((), ()))

SIDES = ((0, -1), (0, 1), (-1, -1), (-1, 1), (1, -1), (1, 1))


def mm(a, b, dims=NN):
    return lax.dot_general(a, b, dims, preferred_element_type=F32)


def split(a):
    high = a.astype(BF16)
    return high, (a - high.astype(F32)).astype(BF16)


def left(a):
    high, low = split(a)
    return jnp.concatenate([high, high, low], axis=1)


def right(b):
    high, low = split(b)
    return jnp.concatenate([high, low, high], axis=0)


def iota(shape, dim):
    return lax.broadcasted_iota(jnp.int32, shape, dim)


def eye_mask(n):
    return iota((n, n), 0) == iota((n, n), 1)


def to_col(row):
    n = row.shape[1]
    return jnp.sum(jnp.where(eye_mask(n), row, 0.0), axis=1, keepdims=True)


def gram(rows):
    high, low = split(rows)
    left = jnp.concatenate([high, high, low], axis=0)
    return mm(left, jnp.concatenate([high, low, high], axis=0), TN)


def full_sum(value):
    return jnp.sum(jnp.sum(value, axis=1, keepdims=True), axis=0, keepdims=True)


def kernel(
    dims,
    feat_in,
    kern_in,
    gain_in,
    bias_in,
    mix_in,
    cot_in,
    mixed_out,
    gfeat_out,
    gmix_out,
    ggain_out,
    gbias_out,
    gker_out,
    gwhite_out,
    feat,
    mix,
    cot,
    kern,
    gain,
    bias,
    tall,
    kpad,
    kst,
    ktst,
    xpad,
    dpad,
    cot2,
    xedge,
    dedge,
    xrows,
    drows,
    xside,
    dside,
    conv,
    alone,
    dact,
    act,
    dnorm,
    gacc,
    bacc,
    kgrad,
    order,
    between,
    mrow,
    mplane,
    mblock,
    msend,
    mrecv,
    mcsend,
    mcrecv,
    send1,
    recv1,
    csend1,
    crecv1,
    cov,
    send2,
    recv2,
    csend2,
    crecv2,
    white,
    send3,
    recv3,
    csend3,
    crecv3,
    gmix,
    send4,
    recv4,
    csend4,
    crecv4,
    gker,
    in_sems,
    hsems,
    rs_s,
    rs_r,
    cx_s,
    cx_r,
    ag_s,
    ag_r,
    mr_s,
    mr_r,
    mc_s,
    mc_r,
):
    ndp, nrow, ncol, height, width = dims
    chans = feat_in.shape[0]
    gwidth = chans // GROUPS
    cells = height * width
    total = cells * nrow * ncol
    chunk = chans // nrow
    nwide = ndp * ncol
    block = 2 * width
    nblk = cells // block
    edge_rows = 2 * height
    middle = slice(width, width + cells)
    dp = lax.axis_index("dp")
    row = lax.axis_index("row")
    col = lax.axis_index("col")

    side = math.isqrt(nrow)
    ys = [lax.rem(row // side + step, side) for step in range(side)]
    xs = [lax.rem(lax.rem(row, side) + step, side) for step in range(side)]
    cs = [lax.rem(col + step, ncol) for step in range(ncol)]
    dps = [lax.rem(dp + step, ndp) for step in range(ndp)]

    def far(*offsets):
        return -sum(min(step, count - step) for step, count in offsets)

    row_order = sorted(
        ((y, x) for y in range(side) for x in range(side) if y + x > 0),
        key=lambda at: far((at[0], side), (at[1], side)),
    )
    wide_order = sorted(
        ((d, c) for d in range(ndp) for c in range(ncol) if d + c > 0),
        key=lambda at: far((at[1], ncol)),
    )
    col_order = [at for at in wide_order if at[0] == 0]
    row_to = [ys[y] * side + xs[x] for y, x in row_order]

    def row_peer(k):
        return (dp, row_to[k], col)

    def col_peer(k):
        return (dp, row, cs[col_order[k][1]])

    def wide_peer(k):
        return (dps[wide_order[k][0]], row, cs[wide_order[k][1]])

    def side_peer(step):
        return (
            dp,
            lax.rem(row + step[0] + nrow, nrow),
            lax.rem(col + step[1] + ncol, ncol),
        )

    arguments = (
        (feat_in, feat),
        (mix_in, mix),
        (cot_in, cot),
        (kern_in, kern),
        (gain_in, gain),
        (bias_in, bias),
    )
    loads = [
        pltpu.make_async_copy(source, target, in_sems.at[i])
        for i, (source, target) in enumerate(arguments)
    ]
    for i in (3, 0, 1, 2, 4, 5):
        loads[i].start()
    def whole(ref, count, send_sem, recv_sem):
        part = ref.at[pl.ds(0, count)]
        return pltpu.make_async_remote_copy(
            src_ref=part,
            dst_ref=part,
            send_sem=send_sem,
            recv_sem=recv_sem,
            device_id=row_peer(0),
            device_id_type=MESH,
        )

    barrier = pltpu.get_barrier_semaphore()

    def greet(peer):
        pl.semaphore_signal(barrier, inc=1, device_id=peer, device_id_type=MESH)

    for k in range(nrow - 1):
        greet(row_peer(k))
    for k in range(nwide - 1):
        greet(wide_peer(k))

    for step in SIDES[2:]:
        greet(side_peer(step))

    lane = iota((chans, width), 1)

    def put(pad, tile, value):
        lanes = pl.ds(pl.multiple_of(tile * width, width), width)
        pad[1, :, lanes] = value.astype(BF16)
        pad[0, :, lanes] = jnp.where(lane == 0, 0.0, pltpu.roll(value, 1, 1)).astype(BF16)
        pad[2, :, lanes] = jnp.where(
            lane == width - 1, 0.0, pltpu.roll(value, width - 1, 1)
        ).astype(BF16)

    def edges(source, edge):
        index = iota((edge_rows, cells), 0)
        cell = jnp.where(index < height, index * width, (index - height) * width + width - 1)
        chosen = (iota((edge_rows, cells), 1) == cell).astype(F32).astype(BF16)
        edge[...] = mm(chosen, source[1, :, middle], NT).astype(BF16)

    def halo_copies(source, edge, rows, sides, base):
        copies = []
        for slot, step in reversed(tuple(enumerate(SIDES))):
            copies.append(
                pltpu.make_async_remote_copy(
                    src_ref=edge,
                    dst_ref=sides.at[slot],
                    send_sem=hsems.at[base + 2],
                    recv_sem=hsems.at[base + 3],
                    device_id=side_peer((-step[0], -step[1])),
                    device_id_type=MESH,
                )
            )
        for slot, (step, lanes) in enumerate(
            (((1, 0), pl.ds(cells, width)), ((-1, 0), pl.ds(width, width)))
        ):
            copies.append(
                pltpu.make_async_remote_copy(
                    src_ref=source.at[1, :, lanes],
                    dst_ref=rows.at[slot],
                    send_sem=hsems.at[base],
                    recv_sem=hsems.at[base + 1],
                    device_id=side_peer(step),
                    device_id_type=MESH,
                )
            )
        for copy in copies:
            copy.start()

    def halo_waits(rows, sides, base):
        return (
            whole(rows, 2, hsems.at[base], hsems.at[base + 1]),
            whole(sides, len(SIDES), hsems.at[base + 2], hsems.at[base + 3]),
        )

    has_up, has_down = row > 0, row < nrow - 1
    has_left, has_right = col > 0, col < ncol - 1

    def side_lanes(sides):
        side_map = sides[...].astype(F32).reshape(8 * edge_rows, chans).T
        at = iota((chans, 8 * edge_rows), 1) // edge_rows
        for slot, step in enumerate(SIDES):
            live = has_left if step[1] < 0 else has_right
            if step[0] < 0:
                live = jnp.logical_and(live, has_up)
            if step[0] > 0:
                live = jnp.logical_and(live, has_down)
            side_map = jnp.where(at == jnp.where(live, -1, slot), 0.0, side_map)
        return jnp.where(at < len(SIDES), side_map, 0.0)

    def bring(side_map, slot, line, first):
        index = slot * edge_rows + line + (height if first else 0)
        shift = (0 if first else width - 1) - index
        return pltpu.roll(side_map, shift % (8 * edge_rows), 1)[:, :width]

    def put_ends(rows, side_map, pad):
        for tile, which, before, after, line, live in (
            (0, 0, 2, 3, height - 1, has_up),
            (height + 1, 1, 4, 5, 0, has_down),
        ):
            value = jnp.where(live, rows[which].astype(F32), 0.0)
            lanes = slice(tile * width, (tile + 1) * width)
            pad[1, :, lanes] = value.astype(BF16)
            pad[0, :, lanes] = jnp.where(
                lane == 0, bring(side_map, before, line, True), pltpu.roll(value, 1, 1)
            ).astype(BF16)
            pad[2, :, lanes] = jnp.where(
                lane == width - 1,
                bring(side_map, after, line, False),
                pltpu.roll(value, width - 1, 1),
            ).astype(BF16)

    def put_columns(side_map, pad, fresh):
        for line in range(height):
            lanes = slice((line + 1) * width, (line + 2) * width)
            if fresh:
                value = pad[1, :, lanes].astype(F32)
                before, after = pltpu.roll(value, 1, 1), pltpu.roll(value, width - 1, 1)
            else:
                before, after = pad[0, :, lanes].astype(F32), pad[2, :, lanes].astype(F32)
            pad[0, :, lanes] = jnp.where(
                lane == 0, bring(side_map, 0, line, True), before
            ).astype(BF16)
            pad[2, :, lanes] = jnp.where(
                lane == width - 1, bring(side_map, 1, line, False), after
            ).astype(BF16)

    def window(pad, tap, start, size):
        shift_row, shift_col = divmod(tap, 3)
        return pad[shift_col, :, pl.ds(pl.multiple_of(start + shift_row * width, width), size)]

    def line_of(index):
        return pl.ds(index, chans, stride=height)

    loads[3].wait()
    kpad[...] = jnp.zeros_like(kpad)
    kpad[: 9 * gwidth] = kern[...]
    own_group = (iota((chans, chans), 0) // gwidth) == (iota((chans, chans), 1) // gwidth)

    def pick(tap):
        tapcol = iota((128, chans), 0)
        within = lax.rem(iota((128, chans), 1), gwidth)
        return (tapcol == 9 * within + tap).astype(F32).astype(BF16)

    @pl.loop(0, 9)
    def _(tap):
        dense = jnp.where(own_group, mm(kpad[...], pick(tap), TN), 0.0)
        kst[:, pl.ds(pl.multiple_of(tap * chans, chans), chans)] = dense.astype(BF16)

    for edge_tile in (slice(0, width), slice(width + cells, 2 * width + cells)):
        xpad[:, :, edge_tile] = jnp.zeros((3, chans, width), BF16)
    loads[0].wait()
    tall[...] = feat[...].astype(F32).reshape(chans * height, width)
    for r in range(height):
        put(xpad, r + 1, tall[line_of(r), :])
    edges(xpad, xedge)
    pl.semaphore_wait(barrier, (nrow - 1) + (nwide - 1) + 4)
    halo_copies(xpad, xedge, xrows, xside, 0)

    @pl.loop(0, nblk)
    def _(n):
        lanes = pl.ds(pl.multiple_of(n * block, block), block)
        taps = [window(xpad, tap, n * block, block) for tap in range(9)]
        alone[:, lanes] = mm(kst[...], jnp.concatenate(taps, axis=0))

    conv[chans:] = jnp.ones((128, cells), BF16)
    for wait in halo_waits(xrows, xside, 0):
        wait.wait_recv()

    side_map1 = side_lanes(xside)
    put_ends(xrows, side_map1, xpad)
    half = width // 2
    first_cols, last_cols = [], []
    for shift_row in range(3):
        for at, base, found in (
            (lane, height, first_cols),
            (lane - half, edge_rows - half, last_cols),
        ):
            source = at + shift_row - 1
            inside = jnp.logical_and(jnp.logical_and(at >= 0, at < height), source >= 0)
            inside = jnp.logical_and(inside, source < height)
            moved = pltpu.roll(side_map1, -(base + shift_row - 1) % width, 1)
            found.append(jnp.where(inside, moved, 0.0).astype(BF16))

    def weights(*taps):
        return jnp.concatenate([kst[:, tap * chans : (tap + 1) * chans] for tap in taps], axis=1)

    def end_rows(tile):
        lanes = slice(tile * width, (tile + 1) * width)
        return jnp.concatenate([xpad[which, :, lanes] for which in range(3)], axis=0)

    upper = mm(weights(0, 1, 2), end_rows(0))
    lower = mm(weights(6, 7, 8), end_rows(height + 1))
    columns = mm(weights(0, 3, 6, 2, 5, 8), jnp.concatenate(first_cols + last_cols, axis=0))
    for r in range(height):
        lanes = slice(r * width, (r + 1) * width)
        value = alone[:, lanes]
        if r == 0:
            value = value + upper
        if r == height - 1:
            value = value + lower
        value = value + jnp.where(lane == 0, pltpu.roll(columns, -r % width, 1), 0.0)
        value = value + jnp.where(
            lane == width - 1, pltpu.roll(columns, (half - 1 - r) % width, 1), 0.0
        )
        conv[:chans, lanes] = value.astype(BF16)

    def all_scattered(red, recv):
        return whole(recv, nrow - 1, rs_s.at[red], rs_r.at[red])

    def all_exchanged(red, crecv):
        return whole(crecv, crecv.shape[0] - 1, cx_s.at[red], cx_r.at[red])

    def all_gathered(red, full):
        return whole(full, chans - chunk, ag_s.at[red], ag_r.at[red])

    def all_spread(red, over_row):
        if over_row:
            return whole(mrecv.at[red], nrow - 1, mr_s.at[red], mr_r.at[red])
        return whole(mcrecv.at[red], ncol - 1, mc_s.at[red], mc_r.at[red])

    def scatter(red, send, recv, k):
        return pltpu.make_async_remote_copy(
            src_ref=send.at[row_to[k]],
            dst_ref=recv.at[k],
            send_sem=rs_s.at[red],
            recv_sem=rs_r.at[red],
            device_id=row_peer(k),
            device_id_type=MESH,
        )

    def scatter_send(red, send, recv):
        for k in range(nrow - 1):
            scatter(red, send, recv, k).start()
        recv[nrow - 1] = send[row]

    def scatter_start(red, send, recv, full):
        send[...] = full.astype(BF16).reshape(send.shape)
        scatter_send(red, send, recv)

    def ordered_sum(slots):
        value = slots[0].astype(F32)
        for j in range(1, slots.shape[0]):
            value = value + slots[j].astype(F32)
        return value

    def scatter_wait(red, send, recv):
        all_scattered(red, recv).wait_recv()
        return ordered_sum(recv)

    def exchange(red, csend, crecv, wide, k, slot):
        return pltpu.make_async_remote_copy(
            src_ref=csend,
            dst_ref=crecv.at[slot],
            send_sem=cx_s.at[red],
            recv_sem=cx_r.at[red],
            device_id=wide_peer(k) if wide else col_peer(k),
            device_id_type=MESH,
        )

    def exchange_start(red, csend, crecv, wide, value):
        mine = dp * ncol + col if wide else col
        csend[...] = value.astype(BF16)
        for k in range(crecv.shape[0] - 1):
            exchange(red, csend, crecv, wide, k, mine).start()
        crecv[mine] = value.astype(BF16)

    def exchange_wait(red, csend, crecv, wide):
        all_exchanged(red, crecv).wait_recv()
        return ordered_sum(crecv)

    def gather(red, full, k, owner):
        rows = pl.ds(pl.multiple_of(owner * chunk, chunk), chunk)
        return pltpu.make_async_remote_copy(
            src_ref=full.at[rows],
            dst_ref=full.at[rows],
            send_sem=ag_s.at[red],
            recv_sem=ag_r.at[red],
            device_id=row_peer(k),
            device_id_type=MESH,
        )

    def gather_start(red, full, value):
        full[pl.ds(pl.multiple_of(row * chunk, chunk), chunk)] = value.astype(BF16)
        for k in range(nrow - 1):
            gather(red, full, k, row).start()

    def gather_wait(red, full):
        all_gathered(red, full).wait_recv()

    def spread(red, over_row, k, slot):
        return pltpu.make_async_remote_copy(
            src_ref=(msend if over_row else mcsend).at[red],
            dst_ref=(mrecv if over_row else mcrecv).at[red, slot],
            send_sem=(mr_s if over_row else mc_s).at[red],
            recv_sem=(mr_r if over_row else mc_r).at[red],
            device_id=row_peer(k) if over_row else col_peer(k),
            device_id_type=MESH,
        )

    def spread_start(red, over_row, value):
        mine = row if over_row else col
        (msend if over_row else mcsend)[red] = value
        for k in range((nrow if over_row else ncol) - 1):
            spread(red, over_row, k, mine).start()
        (mrecv if over_row else mcrecv)[red, mine] = value

    def spread_wait(red, over_row):
        count = nrow if over_row else ncol
        all_spread(red, over_row).wait_recv()
        for j in range(count):
            mrow[j : j + 1] = (mrecv if over_row else mcrecv)[red, j]
        return mrow[:count]

    def planes_copy(k, slot):
        return pltpu.make_async_remote_copy(
            src_ref=mplane,
            dst_ref=mblock.at[slot],
            send_sem=mc_s.at[0],
            recv_sem=mc_r.at[0],
            device_id=col_peer(k),
            device_id_type=MESH,
        )

    def row_sums(source):
        return mm(jnp.ones((16, cells), BF16), source, NT)[:1]

    def centred(both, line):
        sums = jnp.concatenate([both[:, chans:]] * (chans // 128), axis=1)
        return both[:, :chans] - sums * line

    raw = mm(conv[: chans + 16], conv[...], NT)
    local_mean = raw[chans : chans + 1, :chans] * (1.0 / cells)
    scatter_start(0, send1, recv1, centred(raw[:chans], local_mean))
    spread_start(0, True, local_mean)
    for load in loads[4:]:
        load.wait()

    @pl.loop(0, 9)
    def _(tap):
        other = jnp.where(own_group, mm(pick(tap), kpad[...], TN), 0.0)
        ktst[:, pl.ds(pl.multiple_of((8 - tap) * chans, chans), chans)] = other.astype(BF16)

    loads[1].wait()
    loads[2].wait()
    tall[...] = cot[...].astype(F32).reshape(chans * height, width)
    for r in range(height):
        cot2[:, r * width : (r + 1) * width] = tall[line_of(r), :].astype(BF16)

    exchange_start(0, csend1, crecv1, False, scatter_wait(0, send1, recv1))
    mplane[...] = spread_wait(0, True)
    for k in range(ncol - 1):
        planes_copy(k, col).start()
    mblock[col] = mplane[...]
    gather_start(0, cov, exchange_wait(0, csend1, crecv1, False))
    whole(mblock, ncol - 1, mc_s.at[0], mc_r.at[0]).wait_recv()
    means = mblock[...].reshape(nrow * ncol, chans)
    mean = jnp.sum(means, axis=0, keepdims=True) * (1.0 / (nrow * ncol))
    between[...] = gram(means - mean) * float(cells)
    diag = eye_mask(chans)
    gain_col = to_col(gain[...])
    bias_col = to_col(bias[...])
    put_columns(side_map1, xpad, False)

    @pl.loop(0, nblk)
    def _(n):
        lanes = pl.ds(pl.multiple_of(n * block, block), block)
        dact[:, lanes] = mm(mix[...], cot2[:, lanes], TN)

    gather_wait(0, cov)

    covariance = (cov[...].astype(F32) + between[...]) * (1.0 / total) + jnp.where(diag, EPS, 0.0)
    trace = full_sum(jnp.where(diag, covariance, 0.0))
    inv_trace = 1.0 / trace
    inv_root = lax.rsqrt(trace)
    normal = covariance * inv_trace
    normal_r = right(normal)
    normal2 = mm(left(normal), normal_r)
    projs = [jnp.where(diag, 1.5, 0.0) - 0.5 * normal]
    squares = [left(jnp.where(diag, 2.25, 0.0) - 1.5 * normal + 0.25 * normal2)]
    mixes = [right(1.5 * normal - 0.5 * normal2)]
    projs_l, projs_r = [None], [None]
    for k in range(1, NEWTON):
        if k > 1:
            projs_l.append(left(projs[-1]))
            projs_r.append(right(projs[-1]))
            both = mm(projs_l[-1], jnp.concatenate([projs_r[-1], normal_r], axis=1))
            squares.append(left(both[:, :chans]))
            mixes.append(right(both[:, chans:]))
        projs.append(1.5 * projs[-1] - 0.5 * mm(squares[-1], mixes[-1]))
    whiten = projs[-1] * inv_root
    wmean = jnp.sum(whiten * mean, axis=1, keepdims=True)
    whigh, wlow = split(whiten)
    wpair = jnp.concatenate([whigh, wlow], axis=1)

    gain_part, bias_part, product = 0.0, 0.0, 0.0
    for n in range(nblk):
        lanes = slice(n * block, (n + 1) * block)
        here = conv[:chans, lanes]
        normed = mm(wpair, jnp.concatenate([here, here], axis=0)) - wmean
        shifted = gain_col * normed + bias_col
        gate = jax.nn.sigmoid(shifted)
        act[:, lanes] = (shifted * gate).astype(BF16)
        dshift = dact[:, lanes] * gate * (1.0 + shifted * (1.0 - gate))
        grads = (gain_col * dshift).astype(BF16)
        dnorm[:, lanes] = grads
        product = product + mm(grads, conv[:, lanes], NT)
        weighted = dshift * normed
        gain_part = gain_part + weighted[:, :width] + weighted[:, width:]
        bias_part = bias_part + dshift[:, :width] + dshift[:, width:]
    gacc[...] = gain_part
    bacc[...] = bias_part

    scatter_start(1, send2, recv2, centred(product, mean))
    spread_start(1, True, row_sums(dnorm[...]))

    for n in range(nblk):
        for half in range(2):
            r = 2 * n + half
            added = mm(mix[...], act[:, r * width : (r + 1) * width])
            added = added + xpad[1, :, (r + 1) * width : (r + 2) * width].astype(F32)
            tall[line_of(r), :] = added

    exchange_start(1, csend2, crecv2, False, scatter_wait(1, send2, recv2))
    spread_start(1, False, jnp.sum(spread_wait(1, True), axis=0, keepdims=True))
    mixed_out[...] = tall[...].reshape(chans, height, width).astype(BF16)
    send3[...] = mm(cot2[...], act[...], NT).astype(BF16).reshape(send3.shape)
    gather_start(1, white, exchange_wait(1, csend2, crecv2, False))
    grad_sum = jnp.sum(spread_wait(1, False), axis=0, keepdims=True)
    wsum = jnp.sum(whiten * grad_sum, axis=1, keepdims=True) * (1.0 / total)
    gain_sum = jnp.sum(gacc[...], axis=1, keepdims=True)
    bias_sum = jnp.sum(bacc[...], axis=1, keepdims=True)
    gather_wait(1, white)
    scatter_send(2, send3, recv3)

    dwhiten = white[...].astype(F32)
    gwhite_out[...] = dwhiten * (1.0 / float(total) ** 0.5)
    sym = 0.5 * (dwhiten + dwhiten.T)
    sym_r = right(sym)
    cross = mm(left(sym), normal_r)
    dproj = -0.5 * sym
    sym_products = mm(jnp.concatenate(projs_l[1:], axis=0), sym_r)
    for k in range(NEWTON - 1):
        if k == 0:
            dsquare = -0.75 * sym + 0.25 * cross
            dmix = 1.5 * sym - 0.5 * (cross + cross.T)
        else:
            both = mm(left(dproj), jnp.concatenate([projs_r[k], normal_r], axis=1))
            dsquare = both[:, :chans]
            dmix = both[:, chans:] + sym_products[(k - 1) * chans : k * chans]
        dsquare = dsquare + dsquare.T
        change = mm(
            jnp.concatenate([left(dsquare), squares[k]], axis=1),
            jnp.concatenate([mixes[k], right(dmix)], axis=0),
        )
        dproj = 1.5 * dproj - 0.5 * change

    scalar = full_sum(sym * projs[-1]) * 0.5 + full_sum(dproj * normal)
    dsym = (inv_trace * inv_root * (2.0 / total)) * (dproj - jnp.where(diag, scalar, 0.0))
    shift_col = wsum + jnp.sum(dsym * mean, axis=1, keepdims=True)
    dhigh, dlow = split(dsym)
    quad = jnp.concatenate([whigh, wlow, dhigh, dlow], axis=1)

    for n in range(nblk):
        lanes = slice(n * block, (n + 1) * block)
        one, two = dnorm[:, lanes], conv[:chans, lanes]
        value = mm(quad, jnp.concatenate([one, one, two, two], axis=0)) - shift_col
        dpad[1, :, n * block + width : (n + 1) * block + width] = value.astype(BF16)

    turned = dpad[1, :, middle].T

    for tap in range(9):
        dense = mm(window(xpad, tap, 0, cells), turned)
        dense = jnp.where(own_group, dense, 0.0).reshape(GROUPS, gwidth, chans)
        kgrad[tap * gwidth : (tap + 1) * gwidth] = jnp.sum(dense, axis=0)

    kgrad[9 * gwidth :] = jnp.zeros((128 - 9 * gwidth, chans), F32)
    slim = iota((chans, 128), 1)
    grads = jnp.where(slim == 9 * gwidth, gain_sum, kgrad[...].T)
    grads = jnp.where(slim == 9 * gwidth + 1, bias_sum, grads)
    scatter_start(3, send4, recv4, grads)
    scale = 1.0 / float(ndp * total) ** 0.5
    edges(dpad, dedge)
    halo_copies(dpad, dedge, drows, dside, 4)
    exchange_start(2, csend3, crecv3, True, scatter_wait(2, send3, recv3))
    exchange_start(3, csend4, crecv4, True, scatter_wait(3, send4, recv4))
    for wait in halo_waits(drows, dside, 4):
        wait.wait_recv()
    side_map2 = side_lanes(dside)
    put_ends(drows, side_map2, dpad)
    put_columns(side_map2, dpad, True)

    gather_start(2, gmix, exchange_wait(2, csend3, crecv3, True) * scale)

    def back(n):
        lanes = pl.ds(pl.multiple_of(n * block, block), block)
        taps = [window(dpad, tap, n * block, block) for tap in range(9)]
        value = mm(ktst[...], jnp.concatenate(taps, axis=0)) + cot2[:, lanes].astype(F32)
        tall[line_of(2 * n), :] = value[:, :width]
        tall[line_of(2 * n + 1), :] = value[:, width:]

    @pl.loop(0, nblk)
    def _(n):
        back(n)

    gather_start(3, gker, exchange_wait(3, csend4, crecv4, True) * scale)

    gfeat_out[...] = tall[...].reshape(chans, height, width).astype(BF16)
    for wait in halo_waits(xrows, xside, 0) + halo_waits(drows, dside, 4):
        wait.wait_send()
    everything = (
        (send1, recv1, csend1, crecv1, cov),
        (send2, recv2, csend2, crecv2, white),
        (send3, recv3, csend3, crecv3, gmix),
        (send4, recv4, csend4, crecv4, gker),
    )
    for red, (send, recv, csend, crecv, full) in enumerate(everything):
        all_scattered(red, recv).wait_send()
        all_exchanged(red, crecv).wait_send()
        if red < 3:
            all_gathered(red, full).wait_send()
    all_spread(0, True).wait_send()
    all_spread(1, True).wait_send()
    all_spread(1, False).wait_send()
    whole(mblock, ncol - 1, mc_s.at[0], mc_r.at[0]).wait_send()

    gather_wait(2, gmix)
    gmix_out[...] = gmix[...].astype(F32)
    gather_wait(3, gker)
    final = gker[...].astype(F32).T
    for half in range(chans // 128):
        lanes = slice(half * 128, (half + 1) * 128)
        for tap in range(9):
            lines = final[tap * gwidth : (tap + 1) * gwidth, lanes]
            order[half, pl.ds(tap, gwidth, stride=9), :] = lines
        gker_out[:, lanes] = order[half]
    ggain_out[...] = final[9 * gwidth : 9 * gwidth + 1]
    gbias_out[...] = final[9 * gwidth + 1 : 9 * gwidth + 2]
    all_gathered(3, gker).wait_send()


def store(*refs):
    sems = refs[-1]
    count = len(refs) // 2
    copies = [
        pltpu.make_async_copy(refs[i], refs[count + i], sems.at[i]) for i in range(count)
    ]
    for copy in copies:
        copy.start()
    for copy in copies:
        copy.wait()


def solution(mesh):
    ndp, nrow, ncol = (mesh.shape[name] for name in ("dp", "row", "col"))

    def local(features, group_kernel, norm_gain, norm_bias, mix_weight, cotangent):
        chans, height, width = features.shape[1:]
        cells = height * width
        chunk = chans // nrow
        nwide = ndp * ncol
        padded = cells + 2 * width

        def reduction(cols, wide):
            return [
                pltpu.VMEM((nrow, chunk, cols), BF16),
                pltpu.VMEM((nrow, chunk, cols), BF16),
                pltpu.VMEM((chunk, cols), BF16),
                pltpu.VMEM((nwide if wide else ncol, chunk, cols), BF16),
                pltpu.VMEM((chans, cols), BF16),
            ]

        vmem = pl.BlockSpec(memory_space=pltpu.VMEM)
        anywhere = pl.BlockSpec(memory_space=pl.ANY)
        results = (
            ((chans, height, width), BF16),
            ((chans, height, width), BF16),
            ((chans, chans), F32),
            ((1, chans), F32),
            ((1, chans), F32),
            (group_kernel.shape[::-1], F32),
            ((chans, chans), F32),
        )
        outs = pl.pallas_call(
            functools.partial(kernel, (ndp, nrow, ncol, height, width)),
            out_shape=tuple(pltpu.VMEM(shape, dtype) for shape, dtype in results),
            in_specs=[anywhere] * 6,
            out_specs=[vmem] * 7,
            scratch_shapes=[
                pltpu.VMEM((chans, height, width), BF16),
                pltpu.VMEM((chans, chans), BF16),
                pltpu.VMEM((chans, height, width), BF16),
                pltpu.VMEM(group_kernel.shape[::-1], BF16),
                pltpu.VMEM((1, chans), F32),
                pltpu.VMEM((1, chans), F32),
                pltpu.VMEM((chans * height, width), F32),
                pltpu.VMEM((128, chans), BF16),
                pltpu.VMEM((chans, 9 * chans), BF16),
                pltpu.VMEM((chans, 9 * chans), BF16),
                pltpu.VMEM((3, chans, padded), BF16),
                pltpu.VMEM((3, chans, padded), BF16),
                pltpu.VMEM((chans, cells), BF16),
                pltpu.VMEM((2 * height, chans), BF16),
                pltpu.VMEM((2 * height, chans), BF16),
                pltpu.VMEM((2, chans, width), BF16),
                pltpu.VMEM((2, chans, width), BF16),
                pltpu.VMEM((8, 2 * height, chans), BF16),
                pltpu.VMEM((8, 2 * height, chans), BF16),
                pltpu.VMEM((chans + 128, cells), BF16),
                pltpu.VMEM((chans, cells), F32),
                pltpu.VMEM((chans, cells), F32),
                pltpu.VMEM((chans, cells), BF16),
                pltpu.VMEM((chans, cells), BF16),
                pltpu.VMEM((chans, 128), F32),
                pltpu.VMEM((chans, 128), F32),
                pltpu.VMEM((128, chans), F32),
                pltpu.VMEM((chans // 128, group_kernel.shape[1], 128), F32),
                pltpu.VMEM((chans, chans), F32),
                pltpu.VMEM((max(nrow, ncol), chans), F32),
                pltpu.VMEM((nrow, chans), F32),
                pltpu.VMEM((ncol, nrow, chans), F32),
                pltpu.VMEM((2, 1, chans), F32),
                pltpu.VMEM((2, nrow, 1, chans), F32),
                pltpu.VMEM((2, 1, chans), F32),
                pltpu.VMEM((2, ncol, 1, chans), F32),
                *reduction(chans, False),
                *reduction(chans, False),
                *reduction(chans, True),
                *reduction(128, True),
                pltpu.SemaphoreType.DMA((6,)),
                pltpu.SemaphoreType.DMA((8,)),
                *[pltpu.SemaphoreType.DMA((4,))] * 6,
                *[pltpu.SemaphoreType.DMA((2,))] * 4,
            ],
            compiler_params=pltpu.CompilerParams(
                collective_id=0, has_side_effects=True, vmem_limit_bytes=60 * 1024 * 1024
            ),
        )(
            features.reshape(chans, height, width),
            group_kernel.T,
            norm_gain.reshape(1, chans),
            norm_bias.reshape(1, chans),
            mix_weight,
            cotangent.reshape(chans, height, width),
        )
        mixed, gfeat, gmix, ggain, gbias, gker, gwhite = pl.pallas_call(
            store,
            out_shape=tuple(jax.ShapeDtypeStruct(shape, dtype) for shape, dtype in results),
            in_specs=[anywhere] * 7,
            out_specs=[anywhere] * 7,
            scratch_shapes=[pltpu.SemaphoreType.DMA((7,))],
        )(*(pltpu.with_memory_space_constraint(out, pltpu.VMEM) for out in outs))
        return (
            mixed.reshape(features.shape),
            gfeat.reshape(features.shape),
            gmix,
            ggain.reshape(chans),
            gbias.reshape(chans),
            gker.T,
            gwhite[None],
        )

    in_specs = (P("dp", None, "row", "col"), P(), P(), P(), P(), P("dp", None, "row", "col"))
    out_specs = (
        P("dp", None, "row", "col"),
        P("dp", None, "row", "col"),
        P(),
        P(),
        P(),
        P(),
        P("dp", None, None),
    )
    return jax.shard_map(local, mesh=mesh, in_specs=in_specs, out_specs=out_specs, check_vma=False)
```
